32 devices in a mesh: dp: 4 (over z), expert: 8 (over y, x, core).
Axes of the slice: x: 2, y: 2, z: 4, core: 2. Of those that a mesh axis runs over, the one named last changes fastest.
Arguments:
- queries: bfloat16 [8192, 1536], P(('dp', 'expert')), may hold values from -8 to 8
- rotated_key_heads: bfloat16 [8192, 512], P(('dp', 'expert')), may hold values from -8 to 8
- token_value_heads: bfloat16 [8192, 512], P(('dp', 'expert')), may hold values from -4 to 4
- residual: bfloat16 [8192, 1536], P(('dp', 'expert')), may hold values from -20 to 20
- lengths: int32 [32, 4], P(('dp', 'expert')), may hold values from 1 to 128, 256 in all within a row
- request_adapter_index: int32 [128], P(('dp', 'expert')), may hold values from 0 to 63
- attention_output_weight: bfloat16 [1536, 1536], P('dp'), may hold values from -0.15625 to 0.15625
- adapter_down_factor: bfloat16 [64, 1536, 16], P('expert'), may hold values from -0.15625 to 0.15625
- adapter_up_factor: bfloat16 [64, 16, 1536], P('expert'), may hold values from -1.5 to 1.5
- expert_norm_scale: float32 [1536], replicated, may hold values from 0.5 to 1.5
- router_logit_scores: float32 [8192, 8], P(('dp', 'expert')), may hold values from -4 to 404
- routes: int32 [8192, 8], P(('dp', 'expert')), may hold values from 0 to 15, all different within a row; in each aligned block of 256 rows (0 to 255, 256 to 511, ...) at most 160 rows name the same one
- expert_gate_weight: bfloat16 [16, 1536, 512], P('expert'), may hold values from -0.15625 to 0.15625
- expert_up_weight: bfloat16 [16, 1536, 512], P('expert'), may hold values from -0.15625 to 0.15625
- expert_down_weight: bfloat16 [16, 512, 1536], P('expert'), may hold values from -0.25 to 0.25
Outputs:
- block_out: bfloat16 [8192, 1536], P(('dp', 'expert'))
The draws below stay inside these ranges and needn't reach their ends.
Inputs may be any that keep to these rules, and one draw needn't show every extreme that they name: `routes`: in the rows of one device no expert is named by more than 160 rows, a bound that some block reaches.
All inputs are finite; a program needn't handle non-finite values.
Results may differ from the reference program's by a relative error of at most 0.0044.
Values may be sent and summed in bfloat16 or wider, within the bound.
No kernel may reach another device: no remote copies, remote signals or barrier semaphores. Data moves between devices by JAX's collectives and lax.ppermute only.
A program may use at most 128 MiB of HBM per device.

```python
import math
import jax
import jax.numpy as jnp
import numpy as np
from jax import lax

MODEL_WIDTH = 1536
HEADS = 24
KV_HEADS = 8
HEAD = 64
FFE = 512
TOPK = 8
ADAPTER_RANK = 16
ADAPTER_COUNT = 64
TOK_DEV = 256
REQ_DEV = 4
EXPERTS = 16
CAP = 160
TOKENS = 8192
REQUESTS = 128
N_DP = 4
N_EXPERT = 8


def drawn_pair(key):
    base = jax.random.fold_in(key, 7001)
    keys_list = jax.random.split(base, 2)
    groups = HEADS // KV_HEADS
    query_part = jnp.clip(jax.random.normal(keys_list[0], (TOKENS, KV_HEADS, groups, HEAD)), -4.0, 4.0)
    key_part = jnp.clip(jax.random.normal(keys_list[1], (TOKENS, KV_HEADS, HEAD)), -4.0, 4.0)
    return (query_part.reshape(TOKENS, HEADS * HEAD), key_part.reshape(TOKENS, KV_HEADS * HEAD))


def draw_queries(key, part):
    return drawn_pair(key)[0].astype(jnp.bfloat16)


def draw_rotated_key_heads(key, part):
    return drawn_pair(key)[1].astype(jnp.bfloat16)


def draw_residual(key, part):
    keys_list = jax.random.split(jax.random.fold_in(key, 7002), 3)
    row_scale = jnp.exp(jax.random.uniform(keys_list[0], (TOKENS, 1), minval=jnp.log(0.3), maxval=jnp.log(3.0)))
    column_scale = jnp.exp(jax.random.uniform(keys_list[1], (1, MODEL_WIDTH), minval=jnp.log(0.3), maxval=jnp.log(3.0)))
    noise = jnp.clip(0.5 * jax.random.normal(keys_list[2], (TOKENS, MODEL_WIDTH)), -2.0, 2.0)
    return (row_scale * column_scale * noise).astype(jnp.bfloat16)


def draw_router_logit_scores(key, part):
    keys_list = jax.random.split(jax.random.fold_in(key, 7003), 1)
    return jax.random.uniform(keys_list[0], (TOKENS, TOPK), minval=-0.4, maxval=0.4)


def set_ends(array, key, smallest, top_value):
    place = [jax.random.randint(jax.random.fold_in(key, axis), (), 0, length) for axis, length in enumerate(array.shape)]
    widest = array.shape.index(max(array.shape))
    beside = place[:widest] + [(place[widest] + 1) % array.shape[widest]] + place[widest + 1:]
    return array.at[tuple(place)].set(smallest).at[tuple(beside)].set(top_value)


def block_levels(own_key, extent, cuts, least, largest):
    gain, own = 1.0, jax.random.fold_in(own_key, 6)
    for axis_at, blocks in cuts:
        draws = jnp.exp(jax.random.uniform(jax.random.fold_in(own, axis_at), (blocks,), jnp.float32, least / len(cuts), largest / len(cuts)))
        gain = gain * jnp.repeat(draws, extent[axis_at] // blocks).reshape([-1 if axis == axis_at else 1 for axis in range(len(extent))])
    return gain


def split_up(count, total, reach, lean):
    weights = [(1 << 20) // math.isqrt(grade ** lean) + 1 for grade in range(2, count + 1)]
    surplus, holding = total - reach - (count - 1), [1] * (count - 1)
    while surplus > 0:
        movable = [i for i in range(count - 1) if holding[i] < reach]
        whole, left = sum([weights[i] for i in movable]), surplus
        for i in movable:
            extra = min(reach - holding[i], max(1, left * weights[i] // whole), surplus)
            holding[i] = holding[i] + extra
            surplus = surplus - extra
    return np.array([reach] + holding)


def uneven_parts(own_key, amount, total, reach, skew):
    if amount == 2:
        one = jax.random.randint(own_key, (), max(1, total - reach), min(reach, total - 1) + 1)
        return jnp.stack([one, total - one])
    sizes = jnp.asarray(split_up(amount, total, reach, skew), jnp.int32)
    twos = (amount - 1) // 2
    giver, sink = sizes[1:1 + 2 * twos:2], sizes[2:2 + 2 * twos:2]
    margin = jnp.minimum(giver - 1, reach - sink)
    passed = jax.random.randint(jax.random.fold_in(own_key, 1), (twos,), 0, 1 << 20) % (margin + 1)
    sizes = sizes.at[1:1 + 2 * twos:2].set(giver - passed).at[2:2 + 2 * twos:2].set(sink + passed)
    return sizes[jax.random.permutation(jax.random.fold_in(own_key, 2), amount)]


def deal_out(rng, own, number, rows, count, top, reach, slope):
    ranking = jax.random.permutation(rng, count)
    heavy_load, ordinary = load_shares(count, rows * top, reach, slope, True), load_shares(count, rows * top, reach, slope, False)
    places = jnp.arange(count)

    def named(sizes, offset_by):
        used = int((sizes > 0).sum())
        fixed = max(1, used // 4)
        passed = fixed + (places - fixed + offset_by * (used - fixed)) % max(1, count - fixed)
        return jnp.zeros((count,), jnp.int32).at[ranking[jnp.where(places < fixed, places, passed)]].set(jnp.asarray(sizes, jnp.int32))

    sizes = jnp.where(number % 4 == 0, named(heavy_load, number // 4), named(ordinary, number - number // 4 - 1))
    mixed = jax.random.permutation(jax.random.fold_in(own, 3), count)
    giver, receiver = mixed[0:count // 2 * 2:2], mixed[1:count // 2 * 2:2]
    margin = jnp.minimum(sizes[giver] - 1, reach - sizes[receiver]) // 2
    margin = jnp.where((giver == ranking[0]) | (receiver == ranking[0]) | (sizes[receiver] == 0), 0, jnp.maximum(margin, 0))
    passed = jax.random.randint(jax.random.fold_in(own, 4), (count // 2,), 0, 1 << 20) % (margin + 1)
    sizes = sizes.at[giver].add(-passed).at[receiver].add(passed)
    labels = jnp.searchsorted(jnp.cumsum(sizes), jnp.arange(rows * top), side="right").astype(jnp.int32)
    table = labels.reshape(top, rows).T
    table = table[jax.random.permutation(jax.random.fold_in(own, 1), rows)]
    offset_by = jax.random.randint(jax.random.fold_in(own, 2), (rows, 1), 0, top)
    return jnp.take_along_axis(table, (jnp.arange(top)[None, :] + offset_by) % top, axis=1)


def load_shares(number_of, total, bound, skew, full):
    loads = [(1 << 20) // math.isqrt(rank ** skew) + 1 for rank in range(1, number_of + 1)]
    largest = bound if full else min(bound, max(-(-total // number_of), total * loads[0] // sum(loads)))
    least = 1 if total - largest >= number_of - 1 else 0
    holding, spare = [largest] + [least] * (number_of - 1), total - largest - least * (number_of - 1)
    while spare > 0:
        free = [i for i in range(1, number_of) if holding[i] < largest] or [i for i in range(1, number_of) if holding[i] < bound]
        mass, left = sum([loads[i] for i in free]), spare
        for i in free:
            addition = min(bound - holding[i], max(1, left * loads[i] // mass), spare)
            holding[i] = holding[i] + addition
            spare = spare - addition
    return np.array(holding)


def bell_draw(rng, dims, scale, most, shards=(), kind=jnp.bfloat16):
    loudness = block_levels(rng, dims, shards, -0.22, 0.18) if shards else 1.0
    array = jax.random.normal(rng, dims, jnp.float32) * scale * loudness
    return jnp.minimum(jnp.maximum(array, -most), most).astype(kind)


def setup_inputs(seed: int = 0) -> dict:
    arg_keys = jax.random.split(jax.random.key(seed), 16)
    queries = draw_queries(jax.random.fold_in(arg_keys[15], 71), 0)
    rotated_key_heads = draw_rotated_key_heads(jax.random.fold_in(arg_keys[15], 71), 0)
    token_value_heads = bell_draw(arg_keys[2], (TOKENS, KV_HEADS * HEAD), 1.0, 4.0, ((0, 32),))
    residual = draw_residual(jax.random.fold_in(arg_keys[15], 71), 0)
    lengths = jax.vmap(lambda own: uneven_parts(own, REQ_DEV, TOK_DEV, TOK_DEV // 2, 2))(jax.random.split(arg_keys[4], (N_DP * N_EXPERT))).reshape((N_DP * N_EXPERT, REQ_DEV)).astype(jnp.int32)
    request_adapter_index = set_ends(jax.random.randint(arg_keys[5], (REQUESTS,), 0, ADAPTER_COUNT), jax.random.fold_in(arg_keys[5], 1), 0, ADAPTER_COUNT - 1).astype(jnp.int32)
    attention_output_weight = bell_draw(arg_keys[6], (MODEL_WIDTH, MODEL_WIDTH), MODEL_WIDTH ** -0.5, 0.15625, ((0, 4),))
    adapter_down_factor = bell_draw(arg_keys[7], (ADAPTER_COUNT, MODEL_WIDTH, ADAPTER_RANK), MODEL_WIDTH ** -0.5, 0.15625, ((0, 8),))
    adapter_up_factor = bell_draw(arg_keys[8], (ADAPTER_COUNT, ADAPTER_RANK, MODEL_WIDTH), ADAPTER_RANK ** -0.5, 1.5, ((0, 8),))
    expert_norm_scale = jnp.clip(1.0 + 0.1 * jax.random.normal(arg_keys[9], (MODEL_WIDTH,), jnp.float32), 0.5, 1.5)
    router_logit_scores = draw_router_logit_scores(jax.random.fold_in(arg_keys[15], 71), 0)
    routes_keys = jax.random.split(jax.random.fold_in(arg_keys[11], 1), TOKENS // TOK_DEV)
    routes_turns = jax.random.permutation(jax.random.fold_in(arg_keys[11], 3), TOKENS // TOK_DEV)
    routes = jax.vmap(lambda own, number: deal_out(jax.random.fold_in(arg_keys[11], 2), own, number, TOK_DEV, EXPERTS, TOPK, CAP, 1))(routes_keys, routes_turns).reshape((TOKENS, TOPK))
    expert_gate_weight = bell_draw(arg_keys[12], (EXPERTS, MODEL_WIDTH, FFE), MODEL_WIDTH ** -0.5, 0.15625, ((0, 8),))
    expert_up_weight = bell_draw(arg_keys[13], (EXPERTS, MODEL_WIDTH, FFE), MODEL_WIDTH ** -0.5, 0.15625, ((0, 8),))
    expert_down_weight = bell_draw(arg_keys[14], (EXPERTS, FFE, MODEL_WIDTH), FFE ** -0.5, 0.25, ((0, 8),))
    return {"queries": queries, "rotated_key_heads": rotated_key_heads, "token_value_heads": token_value_heads, "residual": residual, "lengths": lengths, "request_adapter_index": request_adapter_index, "attention_output_weight": attention_output_weight, "adapter_down_factor": adapter_down_factor, "adapter_up_factor": adapter_up_factor, "expert_norm_scale": expert_norm_scale, "router_logit_scores": router_logit_scores, "routes": routes, "expert_gate_weight": expert_gate_weight, "expert_up_weight": expert_up_weight, "expert_down_weight": expert_down_weight}


def segment_of(lengths_row):
    request_ends = jnp.cumsum(lengths_row).astype(jnp.int32)
    positions = jnp.arange(TOK_DEV, dtype=jnp.int32)
    return lax.optimization_barrier(jnp.sum((positions[:, None] >= request_ends[None, :]).astype(jnp.int32), axis=1)).astype(jnp.int32)

def attend(queries, rotated_key_heads, token_value_heads, segment):
    groups = HEADS // KV_HEADS
    grouped = queries.astype(jnp.float32).reshape(TOK_DEV, KV_HEADS, groups, HEAD)
    key_heads = rotated_key_heads.astype(jnp.float32).reshape(TOK_DEV, KV_HEADS, HEAD)
    value_heads = token_value_heads.astype(jnp.float32).reshape(TOK_DEV, KV_HEADS, HEAD)
    scores = jnp.einsum('tkgh,skh->kgts', grouped, key_heads) * HEAD ** (-0.5)
    positions = jnp.arange(TOK_DEV, dtype=jnp.int32)
    allowed = (segment[:, None] == segment[None, :]) & (positions[:, None] >= positions[None, :])
    scores = jnp.where(allowed, scores, -1e+30)
    row_peak = lax.optimization_barrier(jnp.max(scores, axis=-1, keepdims=True))
    raised = jnp.exp(scores - row_peak)
    weights = (raised / lax.optimization_barrier(jnp.sum(raised, axis=-1, keepdims=True))).astype(jnp.bfloat16)
    head_mix = jnp.einsum('kgts,skh->tkgh', weights.astype(jnp.float32), value_heads)
    return head_mix.reshape(TOK_DEV, HEADS * HEAD).astype(jnp.bfloat16)

def reference(queries, rotated_key_heads, token_value_heads, residual, lengths, request_adapter_index, attention_output_weight, adapter_down_factor, adapter_up_factor, expert_norm_scale, router_logit_scores, routes, expert_gate_weight, expert_up_weight, expert_down_weight):
    gate_all = expert_gate_weight.astype(jnp.float32)
    up_all = expert_up_weight.astype(jnp.float32)
    down_all = expert_down_weight.astype(jnp.float32)

    def device_part(device_index):
        first_row = device_index * TOK_DEV

        def rows_of(array_in):
            return lax.dynamic_slice_in_dim(array_in, first_row, TOK_DEV, 0)
        segment = segment_of(lengths[device_index])
        ids_row = lax.dynamic_slice_in_dim(request_adapter_index, device_index * REQ_DEV, REQ_DEV, 0)
        context = attend(rows_of(queries), rows_of(rotated_key_heads), rows_of(token_value_heads), segment)
        projected = jnp.dot(context, attention_output_weight, preferred_element_type=jnp.float32)
        adapter_of_token = jnp.take(ids_row, segment).astype(jnp.int32)
        down_factor_rows = jnp.take(adapter_down_factor, adapter_of_token, axis=0).astype(jnp.float32)
        low_rank = jnp.einsum('td,tdk->tk', context.astype(jnp.float32), down_factor_rows).astype(jnp.bfloat16)
        up_factor_rows = jnp.take(adapter_up_factor, adapter_of_token, axis=0).astype(jnp.float32)
        adapter_term = jnp.einsum('tk,tkn->tn', low_rank.astype(jnp.float32), up_factor_rows)
        hidden = rows_of(residual).astype(jnp.float32) + projected + adapter_term
        mean_square = lax.optimization_barrier(jnp.mean(hidden * hidden, axis=-1, keepdims=True))
        normed = (hidden * lax.rsqrt(mean_square + 1e-06) * expert_norm_scale).astype(jnp.bfloat16)
        logits_here = rows_of(router_logit_scores)
        logit_peak = lax.optimization_barrier(jnp.max(logits_here, axis=-1, keepdims=True))
        raised = jnp.exp(logits_here - logit_peak)
        gate_weights = raised / lax.optimization_barrier(jnp.sum(raised, axis=-1, keepdims=True))
        flat_routes = rows_of(routes).reshape(-1)
        route_hits = (flat_routes[:, None] == jnp.arange(EXPERTS, dtype=jnp.int32)[None, :]).astype(jnp.int32)
        slot_rank = lax.optimization_barrier(jnp.sum((jnp.cumsum(route_hits, axis=0).astype(jnp.int32) - route_hits) * route_hits, axis=1)).astype(jnp.int32)
        slot_index = (flat_routes * CAP + slot_rank).astype(jnp.int32)
        anchor = jnp.arange(TOK_DEV * TOPK, dtype=jnp.int32) // TOPK
        sources = jnp.zeros((EXPERTS * CAP,), jnp.int32).at[slot_index].set(anchor)
        filled = jnp.zeros((EXPERTS * CAP,), jnp.int32).at[slot_index].set(1)
        buffer = jnp.where(filled[:, None] > 0, jnp.take(normed, sources, axis=0), jnp.zeros((), normed.dtype))
        buffer = buffer.reshape(EXPERTS, CAP, MODEL_WIDTH).astype(jnp.float32)
        gate_part = jnp.einsum('ecd,edf->ecf', buffer, gate_all)
        up_part = jnp.einsum('ecd,edf->ecf', buffer, up_all)
        active = (jax.nn.silu(gate_part) * up_part).astype(jnp.bfloat16)
        result = jnp.einsum('ecf,efd->ecd', active.astype(jnp.float32), down_all).astype(jnp.bfloat16)
        picked = jnp.take(result.reshape(EXPERTS * CAP, MODEL_WIDTH), slot_index, axis=0).reshape(TOK_DEV, TOPK, MODEL_WIDTH)
        mixture = lax.optimization_barrier(jnp.sum(gate_weights[:, :, None] * picked.astype(jnp.float32), axis=1))
        return (hidden + mixture).astype(jnp.bfloat16)
    blocks = lax.map(device_part, jnp.arange(N_DP * N_EXPERT, dtype=jnp.int32))
    return blocks.reshape(TOKENS, MODEL_WIDTH)
```

```python
import functools

import jax
import jax.numpy as jnp
from jax import lax
from jax.experimental import pallas as pl
from jax.experimental.pallas import tpu as pltpu
from jax.sharding import PartitionSpec as P

HEAD = 64
GROUPS = 3
BF16, F32 = jnp.bfloat16, jnp.float32
VMEM = pl.BlockSpec(memory_space=pltpu.VMEM)
SMEM = pl.BlockSpec(memory_space=pltpu.SMEM)
ANY = pl.BlockSpec(memory_space=pl.ANY)
LIMIT = 56 * 2**20


def call(kernel, name, out_shape, in_specs, out_specs, scratch, flops, moved, **more):
    return pl.pallas_call(
        kernel,
        name=name,
        out_shape=out_shape,
        in_specs=in_specs,
        out_specs=out_specs,
        scratch_shapes=scratch,
        compiler_params=pltpu.CompilerParams(vmem_limit_bytes=LIMIT),
        cost_estimate=pl.CostEstimate(flops=flops, bytes_accessed=moved, transcendentals=0),
        **more,
    )


def attend_kernel(lengths_ref, q_ref, k_ref, v_ref, o_ref, bias):
    tokens = q_ref.shape[0]
    half = tokens // 2

    @pl.when(pl.program_id(0) == 0)
    def _():
        row = lax.broadcasted_iota(jnp.int32, (tokens, tokens), 0)
        col = lax.broadcasted_iota(jnp.int32, (tokens, tokens), 1)
        same = row >= col
        end = 0
        for r in range(lengths_ref.shape[1]):
            end = end + lengths_ref[0, r]
            same = same & ((row < end) | (col >= end))
        bias[...] = jnp.where(same, 0.0, -1e30)

    for j in range(k_ref.shape[1] // HEAD):
        keys = k_ref[:, j * HEAD : (j + 1) * HEAD]
        values = v_ref[:, j * HEAD : (j + 1) * HEAD]
        for g in range(GROUPS):
            at = (j * GROUPS + g) * HEAD
            q = q_ref[:, at : at + HEAD] * jnp.asarray(HEAD**-0.5, BF16)
            for first, seen in ((0, half), (half, tokens)):
                s = lax.dot_general(
                    q[first : first + half],
                    keys[:seen],
                    (((1,), (1,)), ((), ())),
                    preferred_element_type=F32,
                )
                s = s + bias[first : first + half, :seen]
                p = jnp.exp(s - jnp.max(s, axis=-1, keepdims=True))
                w = (p * (1.0 / jnp.sum(p, axis=-1, keepdims=True))).astype(BF16)
                o = jnp.dot(w, values[:seen], preferred_element_type=F32)
                o_ref[first : first + half, at : at + HEAD] = o.astype(BF16)


def attend(lengths, q, k, v):
    tokens, width = q.shape
    pairs = k.shape[1] // (2 * HEAD)
    wide = width // pairs
    return pl.pallas_call(
        attend_kernel,
        name="attend",
        grid=(pairs,),
        out_shape=jax.ShapeDtypeStruct((tokens, width), BF16),
        in_specs=[
            SMEM,
            pl.BlockSpec((tokens, wide), lambda i: (0, i)),
            pl.BlockSpec((tokens, 2 * HEAD), lambda i: (0, i)),
            pl.BlockSpec((tokens, 2 * HEAD), lambda i: (0, i)),
        ],
        out_specs=pl.BlockSpec((tokens, wide), lambda i: (0, i)),
        scratch_shapes=[pltpu.VMEM((tokens, tokens), F32)],
        compiler_params=pltpu.CompilerParams(vmem_limit_bytes=LIMIT),
        cost_estimate=pl.CostEstimate(
            flops=16 * 10**9, bytes_accessed=2 * 10**6, transcendentals=0
        ),
    )(lengths, q, k, v)


def prepare_kernel(logits_ref, routes_ref, down_ref, up_ref, o_ref):
    tokens, top = logits_ref.shape
    logits = logits_ref[...]
    raised = jnp.exp(logits - jnp.max(logits, axis=-1, keepdims=True))
    gates = raised / jnp.sum(raised, axis=-1, keepdims=True)
    lane = lax.broadcasted_iota(jnp.int32, (tokens, 128), 1)
    routes = routes_ref[...]
    gain = jnp.zeros((tokens, 128), F32)
    for j in range(top):
        hit = (lane & 63) == routes[:, j : j + 1]
        gain = gain + jnp.where(hit, gates[:, j : j + 1], 0.0)
    high = gain.astype(BF16).astype(F32)
    count, rank, width = down_ref.shape
    o_ref[:, width:] = jnp.where(lane < 64, high, gain - high).astype(BF16)
    for a in range(count):
        o_ref[2 * rank * a : 2 * rank * a + rank, :width] = down_ref[a]
        o_ref[2 * rank * a + rank : 2 * rank * (a + 1), :width] = up_ref[a]


def prepare(logits, routes, down, up):
    tokens = logits.shape[0]
    width = up.shape[2]
    return call(
        prepare_kernel,
        "prepare",
        jax.ShapeDtypeStruct((tokens, width + 128), BF16),
        [VMEM] * 4,
        VMEM,
        [],
        10**6,
        2 * 10**6,
    )(logits, routes, down, up)


def project_kernel(pools, shards, rank, *refs):
    meta, ids, lengths, ctx_ref, res_ref, scale_ref = refs[:6]
    pool = refs[6 : 6 + pools]
    shard = refs[6 + pools : 6 + pools + shards]
    hidden_ref, normed_ref, low_s, up_s, wo_s, sem_a, sem_w = refs[6 + pools + shards :]
    requests = ids.shape[0]
    tokens, width = res_ref.shape

    def each_shard(do):
        for k in range(shards):
            rows = shard[k].shape[0]
            at = meta[2 * pools + k]

            @pl.when(at >= 0)
            def _():
                do(
                    pltpu.make_async_copy(
                        shard[k], wo_s.at[pl.ds(pl.multiple_of(at, rows), rows)], sem_w.at[k]
                    )
                )

    each_shard(lambda c: c.start())
    for r in range(requests):
        for k in range(pools):
            at = ids[r] - meta[2 * k]

            @pl.when((at >= 0) & (at < meta[2 * k + 1]))
            def _():
                first = pl.multiple_of(at * (2 * rank), 2 * rank)
                for half, to in ((0, low_s), (1, up_s)):
                    pltpu.make_async_copy(
                        pool[k].at[pl.ds(first + half * rank, rank), pl.ds(0, width)],
                        to.at[pl.ds(r * rank, rank)],
                        sem_a.at[r, half],
                    ).start()

    for r in range(requests):
        for half, to in ((0, low_s), (1, up_s)):
            pltpu.make_async_copy(
                pool[0].at[pl.ds(0, rank), pl.ds(0, width)],
                to.at[pl.ds(r * rank, rank)],
                sem_a.at[r, half],
            ).wait()
    ctx = ctx_ref[...]
    low = lax.dot_general(ctx, low_s[...], (((1,), (1,)), ((), ())), preferred_element_type=F32)
    row = lax.broadcasted_iota(jnp.int32, low.shape, 0)
    lane = lax.broadcasted_iota(jnp.int32, low.shape, 1)
    end = 0
    mine = lane < 0
    for r in range(requests):
        start, end = end, end + lengths[0, r]
        inside = (row >= start) & (row < end)
        mine = mine | (inside & (lane >= r * rank) & (lane < (r + 1) * rank))
    low = jnp.where(mine, low, 0.0).astype(BF16)
    hidden_ref[...] = res_ref[...].astype(F32) + jnp.dot(
        low, up_s[...], preferred_element_type=F32
    )
    each_shard(lambda c: c.wait())
    block = min(512, width)
    square = jnp.zeros((tokens, 1), F32)
    for c in range(0, width, block):
        h = hidden_ref[:, c : c + block] + jnp.dot(
            ctx, wo_s[:, c : c + block], preferred_element_type=F32
        )
        hidden_ref[:, c : c + block] = h
        square = square + jnp.sum(h * h, axis=-1, keepdims=True)
    inv = lax.rsqrt(square * (1.0 / width) + 1e-06)
    normed_ref[...] = (hidden_ref[...] * inv * scale_ref[...]).astype(BF16)


def project(meta, ids, lengths, ctx, residual, scale, pools, shards, rank):
    tokens, width = residual.shape
    requests = ids.shape[0]
    return call(
        functools.partial(project_kernel, len(pools), len(shards), rank),
        "project",
        (
            jax.ShapeDtypeStruct((tokens, width), F32),
            jax.ShapeDtypeStruct((tokens, width), BF16),
        ),
        [SMEM] * 3 + [VMEM] * 3 + [ANY] * (len(pools) + len(shards)),
        (VMEM, VMEM),
        [
            pltpu.VMEM((requests * rank, width), BF16),
            pltpu.VMEM((requests * rank, width), BF16),
            pltpu.VMEM((ctx.shape[1], width), BF16),
            pltpu.SemaphoreType.DMA((requests, 2)),
            pltpu.SemaphoreType.DMA((len(shards),)),
        ],
        4 * 10**9,
        10**7,
    )(meta, ids, lengths, ctx, residual, scale, *pools, *shards)


def experts_kernel(groups, blocks, first_ref, *refs):
    xs, gains = refs[:blocks], refs[blocks : 2 * blocks]
    w = refs[2 * blocks : 2 * blocks + 3 * groups]
    outs = refs[2 * blocks + 3 * groups : 3 * blocks + 3 * groups]
    held, strips = refs[3 * blocks + 3 * groups : -3], refs[-3]
    sem, sem_g = refs[-2:]
    local = w[0].shape[0]
    total = groups * local
    last = gains[0].shape[1] - 128
    pulls = [
        pltpu.make_async_copy(gains[b].at[:, pl.ds(last, 128)], strips.at[b], sem_g.at[b])
        for b in range(blocks)
    ]
    for p in pulls:
        p.start()

    def fetch(e):
        return [
            pltpu.make_async_copy(w[3 * (e // local) + k].at[e % local], held[k].at[e], sem.at[e, k])
            for k in range(3)
        ]

    for e in range(min(2, total)):
        for c in fetch(e):
            c.start()
    for e in range(total):
        copies = fetch(e)
        copies[0].wait()
        copies[1].wait()
        for b in range(blocks):
            x = xs[b][...]
            if e == 0:
                pulls[b].wait()
            gain = strips[b].astype(F32)
            lane = lax.broadcasted_iota(jnp.int32, gain.shape, 1)
            coef = jnp.sum(
                jnp.where((lane & 63) == first_ref[e], gain, 0.0), axis=-1, keepdims=True
            )
            gate = jnp.dot(x, held[0][e], preferred_element_type=F32)
            up = jnp.dot(x, held[1][e], preferred_element_type=F32)
            act = (gate / (1.0 + jnp.exp(-gate)) * up * coef).astype(BF16)
            if b == 0:
                copies[2].wait()
                if e + 2 < total:
                    for c in fetch(e + 2):
                        c.start()
            down = jnp.dot(act, held[2][e], preferred_element_type=F32)
            if total == 1:
                outs[b][...] = down.astype(BF16)
            elif e == 0:
                held[3][b] = down
            elif e < total - 1:
                held[3][b] += down
            else:
                outs[b][...] = (held[3][b] + down).astype(BF16)


def run_experts(numbers, xs, gains, weights):
    groups, blocks = len(weights) // 3, len(xs)
    tokens, width = xs[0].shape
    local, _, hid = weights[0].shape
    total = groups * local
    out = jax.ShapeDtypeStruct((tokens, width), BF16)
    return call(
        functools.partial(experts_kernel, groups, blocks),
        "experts",
        (out,) * blocks,
        [SMEM] + [VMEM] * blocks + [ANY] * blocks + [ANY] * (3 * groups),
        (VMEM,) * blocks,
        [
            pltpu.VMEM((total, width, hid), BF16),
            pltpu.VMEM((total, width, hid), BF16),
            pltpu.VMEM((total, hid, width), BF16),
            pltpu.VMEM((blocks, tokens, width), F32),
            pltpu.VMEM((blocks, tokens, 128), BF16),
            pltpu.SemaphoreType.DMA((total, 3)),
            pltpu.SemaphoreType.DMA((blocks,)),
        ],
        6 * blocks * tokens * width * hid * total,
        6 * total * width * hid,
    )(numbers, *xs, *gains, *weights)


def per_device(
    queries,
    rotated_key_heads,
    token_value_heads,
    residual,
    lengths,
    request_adapter_index,
    attention_output_weight,
    adapter_down_factor,
    adapter_up_factor,
    expert_norm_scale,
    router_logit_scores,
    routes,
    expert_gate_weight,
    expert_up_weight,
    expert_down_weight,
):
    tokens = queries.shape[0]
    rank = adapter_up_factor.shape[1]
    held_adapters = adapter_up_factor.shape[0]
    local = expert_gate_weight.shape[0]
    n_dp, n_ex = lax.axis_size("dp"), lax.axis_size("expert")
    z, i = lax.axis_index("dp"), lax.axis_index("expert")
    rows = attention_output_weight.shape[0]
    both = ("dp", "expert")
    down_t = jnp.swapaxes(adapter_down_factor, 1, 2)
    scale = expert_norm_scale.reshape(1, -1)
    weights = (expert_gate_weight, expert_up_weight, expert_down_weight)
    paired = n_ex == 8 and held_adapters * 2 * rank == tokens

    context = attend(lengths, queries, rotated_key_heads, token_value_heads)

    if not paired:
        padded = tokens
        packed = prepare_any(router_logit_scores, routes, down_t, adapter_up_factor)
        gains, pool = packed
        shard = lax.all_gather(attention_output_weight, "dp", axis=0, tiled=True)
        pool = lax.all_gather(pool, "expert", axis=0, tiled=True)
        meta = jnp.stack([0 * z, 0 * z + held_adapters * n_ex, 0 * z])
        hidden, normed = project(
            meta, request_adapter_index, lengths, context, residual, scale, [pool], [shard], rank
        )
        every = lax.all_gather(normed, "expert", axis=0, tiled=True)
        every_gain = lax.all_gather(gains, "expert", axis=0, tiled=True)
        numbers = i * local + jnp.arange(local, dtype=jnp.int32)
        parts = [
            run_experts(
                numbers,
                [every[d * padded : (d + 1) * padded]],
                [every_gain[d * padded : (d + 1) * padded]],
                weights,
            )[0]
            for d in range(n_ex)
        ]
        mixture = lax.psum_scatter(
            jnp.concatenate(parts, axis=0), "expert", scatter_dimension=0, tiled=True
        )
        return (hidden + mixture.astype(F32)).astype(BF16)

    def beside(a):
        return lax.ppermute(a, "expert", [(e, e ^ 1) for e in range(n_ex)])

    def across(a):
        return lax.ppermute(a, "expert", [(e, e ^ (4 if e & 1 else 2)) for e in range(n_ex)])

    def along(a, step):
        pairs = []
        for e in range(n_ex):
            for d in range(n_dp):
                to = d - 1 if e & 1 else d + 1
                origin = d + step - 1 if e & 1 else d - step + 1
                if 0 <= to < n_dp and 0 <= origin < n_dp:
                    pairs.append((d * n_ex + e, to * n_ex + e))
        return lax.ppermute(a, both, pairs)

    own = prepare(router_logit_scores, routes, down_t, adapter_up_factor)
    pair_weights = tuple(beside(w) for w in weights)
    p0 = across(own)
    other = beside(own)
    p1 = across(other)
    p0_other = beside(p0)
    p2 = across(p0_other)
    p1_other, p2_other = beside(p1), beside(p2)
    shards, at = [attention_output_weight], [z * rows]
    up_side = 1 - 2 * (i & 1)
    moving = attention_output_weight
    for step in range(1, n_dp):
        moving = along(moving, step)
        for piece, source in ((moving, z - up_side * step), (beside(moving), z + up_side * step)):
            shards.append(piece)
            at.append(jnp.where((source >= 0) & (source < n_dp), source * rows, -1))
    c = i & 1
    near = i ^ jnp.where(c == 0, 2, 4)
    near_other = i ^ jnp.where(c == 0, 4, 2)
    owners = [i, i ^ 1, near, near ^ 1, near_other ^ 1, near_other, i ^ 7, i ^ 6]
    pools = [own, other, p0, p1, p0_other, p1_other, p2, p2_other]
    meta = jnp.stack(
        [v for o in owners for v in (o * held_adapters, 0 * o + held_adapters)] + at
    )
    hidden, normed = project(
        meta, request_adapter_index, lengths, context, residual, scale, pools, shards, rank
    )
    b0 = across(normed)
    b1 = across(beside(normed))
    far = across(beside(b0))
    mine = (i - c) * local
    order = jnp.arange(local, dtype=jnp.int32)
    numbers = jnp.concatenate([mine + c * local + order, mine + (1 - c) * local + order])
    run = functools.partial(run_experts, numbers, weights=weights + pair_weights)
    (home,) = run([normed], [own])
    r0, r1 = run([b0, b1], [p0, p1])
    (r_far,) = run([far], [p2])
    back1 = beside(across(r1))
    via = beside(across(r_far))
    back0 = across((r0.astype(F32) + via.astype(F32)).astype(BF16))
    mixture = home.astype(F32) + back0.astype(F32) + back1.astype(F32)
    return (hidden + mixture).astype(BF16)


def prepare_any_kernel(logits_ref, routes_ref, down_ref, up_ref, gain_ref, pool_ref):
    tokens, top = logits_ref.shape
    logits = logits_ref[...]
    raised = jnp.exp(logits - jnp.max(logits, axis=-1, keepdims=True))
    gates = raised / jnp.sum(raised, axis=-1, keepdims=True)
    lane = lax.broadcasted_iota(jnp.int32, (tokens, 128), 1)
    routes = routes_ref[...]
    gain = jnp.zeros((tokens, 128), F32)
    for j in range(top):
        hit = (lane & 63) == routes[:, j : j + 1]
        gain = gain + jnp.where(hit, gates[:, j : j + 1], 0.0)
    high = gain.astype(BF16).astype(F32)
    gain_ref[...] = jnp.where(lane < 64, high, gain - high).astype(BF16)
    count, rank, _ = down_ref.shape
    for a in range(count):
        pool_ref[2 * rank * a : 2 * rank * a + rank] = down_ref[a]
        pool_ref[2 * rank * a + rank : 2 * rank * (a + 1)] = up_ref[a]


def prepare_any(logits, routes, down, up):
    count, rank, width = up.shape
    return call(
        prepare_any_kernel,
        "prepare_any",
        (
            jax.ShapeDtypeStruct((logits.shape[0], 128), BF16),
            jax.ShapeDtypeStruct((2 * rank * count, width), BF16),
        ),
        [VMEM] * 4,
        (VMEM, VMEM),
        [],
        10**6,
        2 * 10**6,
    )(logits, routes, down, up)


def solution(mesh):
    return jax.shard_map(
        per_device,
        mesh=mesh,
        in_specs=(
            P(("dp", "expert"), None),
            P(("dp", "expert"), None),
            P(("dp", "expert"), None),
            P(("dp", "expert"), None),
            P(("dp", "expert"), None),
            P(("dp", "expert")),
            P("dp", None),
            P("expert", None, None),
            P("expert", None, None),
            P(),
            P(("dp", "expert"), None),
            P(("dp", "expert"), None),
            P("expert", None, None),
            P("expert", None, None),
            P("expert", None, None),
        ),
        out_specs=P(("dp", "expert"), None),
        check_vma=False,
    )
```

```python
import functools

import jax
import jax.numpy as jnp
from jax import lax
from jax.experimental import pallas as pl
from jax.experimental.pallas import tpu as pltpu
from jax.sharding import PartitionSpec as P

HEAD = 64
GROUPS = 3
BF16, F32 = jnp.bfloat16, jnp.float32
VMEM = pl.BlockSpec(memory_space=pltpu.VMEM)
SMEM = pl.BlockSpec(memory_space=pltpu.SMEM)
ANY = pl.BlockSpec(memory_space=pl.ANY)
MIB = 2**20


def call(kernel, name, out_shape, in_specs, out_specs, scratch, room, flops, **more):
    return pl.pallas_call(
        kernel,
        name=name,
        out_shape=out_shape,
        in_specs=in_specs,
        out_specs=out_specs,
        scratch_shapes=scratch,
        compiler_params=pltpu.CompilerParams(vmem_limit_bytes=room * MIB),
        cost_estimate=pl.CostEstimate(flops=flops, bytes_accessed=MIB, transcendentals=0),
        **more,
    )


def attend_kernel(lengths_ref, q_ref, k_ref, v_ref, o_ref, bias):
    tokens = q_ref.shape[0]
    half = tokens // 2

    @pl.when(pl.program_id(0) == 0)
    def _():
        row = lax.broadcasted_iota(jnp.int32, (tokens, tokens), 0)
        col = lax.broadcasted_iota(jnp.int32, (tokens, tokens), 1)
        same = row >= col
        end = 0
        for r in range(lengths_ref.shape[1]):
            end = end + lengths_ref[0, r]
            same = same & ((row < end) | (col >= end))
        bias[...] = jnp.where(same, 0.0, -1e30)

    for j in range(k_ref.shape[1] // HEAD):
        keys = k_ref[:, j * HEAD : (j + 1) * HEAD]
        values = v_ref[:, j * HEAD : (j + 1) * HEAD]
        for g in range(GROUPS):
            at = (j * GROUPS + g) * HEAD
            q = q_ref[:, at : at + HEAD] * jnp.asarray(HEAD**-0.5, BF16)
            for first, seen in ((0, half), (half, tokens)):
                s = lax.dot_general(
                    q[first : first + half],
                    keys[:seen],
                    (((1,), (1,)), ((), ())),
                    preferred_element_type=F32,
                )
                s = s + bias[first : first + half, :seen]
                p = jnp.exp(s - jnp.max(s, axis=-1, keepdims=True))
                w = (p * (1.0 / jnp.sum(p, axis=-1, keepdims=True))).astype(BF16)
                o = jnp.dot(w, values[:seen], preferred_element_type=F32)
                o_ref[first : first + half, at : at + HEAD] = o.astype(BF16)


def attend(lengths, q, k, v, first, pairs):
    tokens = q.shape[0]
    wide = 2 * GROUPS * HEAD
    return pl.pallas_call(
        attend_kernel,
        name="attend",
        grid=(pairs,),
        out_shape=jax.ShapeDtypeStruct((tokens, wide * pairs), BF16),
        in_specs=[
            SMEM,
            pl.BlockSpec((tokens, wide), lambda i: (0, first + i)),
            pl.BlockSpec((tokens, 2 * HEAD), lambda i: (0, first + i)),
            pl.BlockSpec((tokens, 2 * HEAD), lambda i: (0, first + i)),
        ],
        out_specs=pl.BlockSpec((tokens, wide), lambda i: (0, i)),
        scratch_shapes=[pltpu.VMEM((tokens, tokens), F32)],
        compiler_params=pltpu.CompilerParams(vmem_limit_bytes=8 * MIB),
        cost_estimate=pl.CostEstimate(flops=10**9, bytes_accessed=MIB, transcendentals=0),
    )(lengths, q, k, v)


def prepare_kernel(logits_ref, routes_ref, down_ref, up_ref, gain_ref, pool_ref):
    top, tokens = logits_ref.shape
    logits = logits_ref[...]
    raised = jnp.exp(logits - jnp.max(logits, axis=0, keepdims=True))
    gates = raised / jnp.sum(raised, axis=0, keepdims=True)
    expert = lax.broadcasted_iota(jnp.int32, (64, tokens), 0)
    gain = jnp.zeros((64, tokens), F32)
    for j in range(top):
        gain = gain + jnp.where(expert == routes_ref[j : j + 1], gates[j : j + 1], 0.0)
    high = gain.astype(BF16).astype(F32)
    gain_ref[...] = jnp.concatenate([high, gain - high], axis=0).T.astype(BF16)
    count, rank, _ = down_ref.shape
    for a in range(count):
        pool_ref[2 * rank * a : 2 * rank * a + rank] = down_ref[a]
        pool_ref[2 * rank * a + rank : 2 * rank * (a + 1)] = up_ref[a]


def prepare_joined_kernel(logits_ref, routes_ref, down_ref, up_ref, o_ref):
    width = down_ref.shape[2]
    prepare_kernel(
        logits_ref, routes_ref, down_ref, up_ref, o_ref.at[:, width:], o_ref.at[:, :width]
    )


def prepare(logits, routes, down, up, joined):
    tokens = logits.shape[1]
    count, rank, width = up.shape
    apart = (
        jax.ShapeDtypeStruct((tokens, 128), BF16),
        jax.ShapeDtypeStruct((2 * rank * count, width), BF16),
    )
    return call(
        prepare_joined_kernel if joined else prepare_kernel,
        "prepare",
        jax.ShapeDtypeStruct((tokens, width + 128), BF16) if joined else apart,
        [VMEM] * 4,
        VMEM if joined else (VMEM, VMEM),
        [],
        4,
        10**6,
    )(logits, routes, down, up)


def each_shard(starts, shard, wo_s, sem, do):
    for k, at in enumerate(starts):
        rows = shard[k].shape[0]

        @pl.when(at >= 0)
        def _():
            to = wo_s.at[pl.ds(pl.multiple_of(at, rows), rows)]
            do(pltpu.make_async_copy(shard[k], to, sem.at[k]))


def project_kernel(owners, sources, rank, held, *refs):
    pools, shards = len(owners), len(sources)
    ids, lengths, res_ref = refs[:3]
    ctx = refs[3:-5 - 1 - pools - shards]
    pool = refs[-6 - pools - shards : -6 - shards]
    shard = refs[-6 - shards : -6]
    hidden_ref, low_s, up_s, wo_s, sem_a, sem_w = refs[-6:]
    requests = ids.shape[0]
    tokens, width = res_ref.shape
    z, i = lax.axis_index("dp"), lax.axis_index("expert")
    starts = [f(z, i) for f in sources]
    each_shard(starts, shard, wo_s, sem_w, lambda c: c.start())
    for r in range(requests):
        for k in range(pools):
            at = ids[r] - owners[k](i) * held

            @pl.when((at >= 0) & (at < pool[k].shape[0] // (2 * rank)))
            def _():
                first = pl.multiple_of(at * (2 * rank), 2 * rank)
                for half, to in ((0, low_s), (1, up_s)):
                    pltpu.make_async_copy(
                        pool[k].at[pl.ds(first + half * rank, rank), pl.ds(0, width)],
                        to.at[pl.ds(r * rank, rank)],
                        sem_a.at[r, half],
                    ).start()

    for r in range(requests):
        for half, to in ((0, low_s), (1, up_s)):
            pltpu.make_async_copy(
                pool[0].at[pl.ds(0, rank), pl.ds(0, width)],
                to.at[pl.ds(r * rank, rank)],
                sem_a.at[r, half],
            ).wait()
    low, at = 0.0, 0
    for c in ctx:
        low = low + lax.dot_general(
            c[...],
            low_s[:, at : at + c.shape[1]],
            (((1,), (1,)), ((), ())),
            preferred_element_type=F32,
        )
        at += c.shape[1]
    row = lax.broadcasted_iota(jnp.int32, low.shape, 0)
    lane = lax.broadcasted_iota(jnp.int32, low.shape, 1)
    end = 0
    mine = lane < 0
    for r in range(requests):
        start, end = end, end + lengths[0, r]
        inside = (row >= start) & (row < end)
        mine = mine | (inside & (lane >= r * rank) & (lane < (r + 1) * rank))
    low = jnp.where(mine, low, 0.0).astype(BF16)
    hidden_ref[...] = res_ref[...].astype(F32) + jnp.dot(
        low, up_s[...], preferred_element_type=F32
    )
    each_shard(starts, shard, wo_s, sem_w, lambda c: c.wait())
    for at, piece in zip(starts, shard):
        add_shard(at, piece.shape[0], ctx, wo_s, hidden_ref)


def add_shard(at, rows, ctx, wo_s, hidden_ref):
    covered = 0
    for c in ctx:
        wide = min(rows, c.shape[1])
        for first in range(0, c.shape[1], wide):

            @pl.when((at >= 0) & (covered + first >= at) & (covered + first < at + rows))
            def _():
                hidden_ref[...] += jnp.dot(
                    c[:, first : first + wide],
                    wo_s[covered + first : covered + first + wide],
                    preferred_element_type=F32,
                )

        covered += c.shape[1]


def project(ids, lengths, ctx, residual, pools, owners, shards, sources, rank, held):
    tokens, width = residual.shape
    requests = ids.shape[0]
    return call(
        functools.partial(project_kernel, owners, sources, rank, held),
        "project",
        jax.ShapeDtypeStruct((tokens, width), F32),
        [SMEM] * 2 + [VMEM] * (1 + len(ctx)) + [ANY] * (len(pools) + len(shards)),
        VMEM,
        [
            pltpu.VMEM((requests * rank, width), BF16),
            pltpu.VMEM((requests * rank, width), BF16),
            pltpu.VMEM((width, width), BF16),
            pltpu.SemaphoreType.DMA((requests, 2)),
            pltpu.SemaphoreType.DMA((len(shards),)),
        ],
        12,
        10**9,
    )(ids, lengths, residual, *ctx, *pools, *shards)


def normalise_kernel(sources, *refs):
    shards = len(sources)
    scale_ref, part_ref = refs[:2]
    if shards:
        ctx, shard = refs[2 : -4 - shards], refs[-4 - shards : -4]
        hidden_ref, normed_ref, wo_s, sem = refs[-4:]
        z, i = lax.axis_index("dp"), lax.axis_index("expert")
        starts = [f(z, i) for f in sources]
        each_shard(starts, shard, wo_s, sem, lambda c: c.start())
    else:
        hidden_ref, normed_ref = refs[-2:]
    hidden_ref[...] = part_ref[...]
    if shards:
        each_shard(starts, shard, wo_s, sem, lambda c: c.wait())
        for at, piece in zip(starts, shard):
            add_shard(at, piece.shape[0], ctx, wo_s, hidden_ref)
    h = hidden_ref[...]
    width = h.shape[1]
    inv = lax.rsqrt(jnp.sum(h * h, axis=-1, keepdims=True) * (1.0 / width) + 1e-06)
    normed_ref[...] = (h * inv * scale_ref[...].reshape(1, width)).astype(BF16)


def normalise(scale, part, ctx, shards, sources):
    tokens, width = part.shape
    extra = [pltpu.VMEM((width, width), BF16), pltpu.SemaphoreType.DMA((len(shards),))]
    more = (*ctx, *shards) if shards else ()
    return call(
        functools.partial(normalise_kernel, sources),
        "normalise",
        (
            jax.ShapeDtypeStruct((tokens, width), F32),
            jax.ShapeDtypeStruct((tokens, width), BF16),
        ),
        [VMEM] * 2 + ([VMEM] * len(ctx) + [ANY] * len(shards) if shards else []),
        (VMEM, VMEM),
        extra if shards else [],
        12,
        10**8,
    )(scale, part, *more)


def experts_kernel(groups, spread, x_ref, gain_ref, *refs):
    w, out_ref = refs[: 3 * groups], refs[3 * groups]
    total_ref, strip, sem = refs[3 * groups + 1 :]
    local = w[0].shape[0]
    total = groups * local
    pull = pltpu.make_async_copy(
        gain_ref.at[:, pl.ds(gain_ref.shape[1] - 128, 128)], strip, sem
    )
    pull.start()
    i = lax.axis_index("expert")
    x = x_ref[...]
    for e in range(total):
        g, own = divmod(e, local)
        gate = jnp.dot(x, w[3 * g][own], preferred_element_type=F32)
        up = jnp.dot(x, w[3 * g + 1][own], preferred_element_type=F32)
        if e == 0:
            pull.wait()
        number = spread(i, g) * local + own
        gain = strip[...].astype(F32)
        lane = lax.broadcasted_iota(jnp.int32, gain.shape, 1)
        coef = jnp.sum(jnp.where((lane & 63) == number, gain, 0.0), axis=-1, keepdims=True)
        act = (gate / (1.0 + jnp.exp(-gate)) * up * coef).astype(BF16)
        down = jnp.dot(act, w[3 * g + 2][own], preferred_element_type=F32)
        if total == 1:
            out_ref[...] = down.astype(BF16)
        elif e == 0:
            total_ref[...] = down
        elif e < total - 1:
            total_ref[...] += down
        else:
            out_ref[...] = (total_ref[...] + down).astype(BF16)


def run_experts(x, gain, weights, spread):
    groups = len(weights) // 3
    tokens, width = x.shape
    return call(
        functools.partial(experts_kernel, groups, spread),
        "experts",
        jax.ShapeDtypeStruct((tokens, width), BF16),
        [VMEM, ANY] + [VMEM] * (3 * groups),
        VMEM,
        [
            pltpu.VMEM((tokens, width), F32),
            pltpu.VMEM((tokens, 128), BF16),
            pltpu.SemaphoreType.DMA,
        ],
        12,
        10**9,
    )(x, gain, *weights)


def per_device(
    queries,
    rotated_key_heads,
    token_value_heads,
    residual,
    lengths,
    request_adapter_index,
    attention_output_weight,
    adapter_down_factor,
    adapter_up_factor,
    expert_norm_scale,
    router_logit_scores,
    routes,
    expert_gate_weight,
    expert_up_weight,
    expert_down_weight,
):
    tokens = queries.shape[0]
    rank = adapter_up_factor.shape[1]
    held = adapter_up_factor.shape[0]
    n_dp, n_ex = lax.axis_size("dp"), lax.axis_size("expert")
    rows, width = attention_output_weight.shape
    down_t = jnp.swapaxes(adapter_down_factor, 1, 2)
    weights = (expert_gate_weight, expert_up_weight, expert_down_weight)
    paired = n_ex == 8 and held * 2 * rank == tokens
    qkv = (lengths, queries, rotated_key_heads, token_value_heads)
    pairs = rotated_key_heads.shape[1] // (2 * HEAD)
    known = (request_adapter_index, lengths)
    packed = prepare(router_logit_scores.T, routes.T, down_t, adapter_up_factor, paired)

    if not paired:
        gains, pool = packed
        context = [attend(*qkv, 0, pairs)]
        shard = lax.all_gather(attention_output_weight, "dp", axis=0, tiled=True)
        pool = lax.all_gather(pool, "expert", axis=0, tiled=True)
        part = project(
            *known,
            context,
            residual,
            [pool],
            [lambda i: 0],
            [shard],
            [lambda z, i: z * 0],
            rank,
            held,
        )
        hidden, normed = normalise(expert_norm_scale, part, context, [], [])
        every = lax.all_gather(normed, "expert", axis=0, tiled=True)
        every_gain = lax.all_gather(gains, "expert", axis=0, tiled=True)
        parts = [
            run_experts(
                every[d * tokens : (d + 1) * tokens],
                every_gain[d * tokens : (d + 1) * tokens],
                weights,
                lambda i, g: i,
            )
            for d in range(n_ex)
        ]
        mixture = lax.psum_scatter(
            jnp.concatenate(parts, axis=0), "expert", scatter_dimension=0, tiled=True
        )
        return (hidden + mixture.astype(F32)).astype(BF16)

    def beside(a):
        return lax.ppermute(a, "expert", [(e, e ^ 1) for e in range(n_ex)])

    def across(a):
        return lax.ppermute(a, "expert", [(e, e ^ (4 if e & 1 else 2)) for e in range(n_ex)])

    def along(a, step):
        sent = []
        for e in range(n_ex):
            for d in range(n_dp):
                to = d - 1 if e & 1 else d + 1
                origin = d + step - 1 if e & 1 else d - step + 1
                if 0 <= to < n_dp and 0 <= origin < n_dp:
                    sent.append((d * n_ex + e, to * n_ex + e))
        return lax.ppermute(a, ("dp", "expert"), sent)

    def after(a, *others):
        return lax.optimization_barrier((a, *others))[0]

    def first_row(step, side):
        def at(z, i):
            source = z + side * step * (1 - 2 * (i & 1))
            return jnp.where((source >= 0) & (source < n_dp), source * rows, -1)

        return at

    own = packed
    z1 = along(attention_output_weight, 1)
    p0 = across(own)
    other = beside(own)
    p1 = across(other)
    half = pairs // 2
    ctx0 = attend(*qkv, 0, half)
    z2 = along(after(z1, ctx0), 2)
    p0_other = beside(after(p0, ctx0))
    p2 = across(p0_other)
    pair_weights = tuple(beside(after(w, p0_other)) for w in weights)
    ctx1 = attend(*qkv, half, pairs - half)
    z3 = along(after(z2, ctx1), 3)
    p1_other, p2_other = beside(p1), beside(p2)
    z1_other, z2_other, z3_other = beside(z1), beside(z2), beside(z3)
    context = [ctx0, ctx1]
    owners = [
        lambda i: i,
        lambda i: i ^ 1,
        lambda i: i ^ (2 + 2 * (i & 1)),
        lambda i: i ^ (3 + 2 * (i & 1)),
        lambda i: i ^ (5 - 2 * (i & 1)),
        lambda i: i ^ (4 - 2 * (i & 1)),
        lambda i: i ^ 7,
        lambda i: i ^ 6,
    ]
    part = project(
        *known,
        context,
        residual,
        [own, other, p0, p1, p0_other, p1_other, p2, p2_other],
        owners,
        [attention_output_weight, z1, z1_other, z2, z2_other],
        [lambda z, i: z * rows] + [first_row(s, side) for s in (1, 2) for side in (-1, 1)],
        rank,
        held,
    )
    hidden, normed = normalise(
        expert_norm_scale, part, context, [z3, z3_other], [first_row(3, -1), first_row(3, 1)]
    )
    b0 = across(normed)
    b1 = across(beside(normed))
    run = functools.partial(
        run_experts, weights=weights + pair_weights, spread=lambda i, g: i ^ g
    )
    home = run(normed, own)
    far = across(beside(after(b0, home)))
    r0 = run(after(b0, home), p0)
    r1 = run(after(b1, r0), p1)
    back1 = beside(across(r1))
    r_far = run(after(far, r1), p2)
    via = beside(across(r_far))
    back0 = across((r0.astype(F32) + via.astype(F32)).astype(BF16))
    mixture = home.astype(F32) + back0.astype(F32) + back1.astype(F32)
    return (hidden + mixture).astype(BF16)


def solution(mesh):
    return jax.shard_map(
        per_device,
        mesh=mesh,
        in_specs=(
            P(("dp", "expert"), None),
            P(("dp", "expert"), None),
            P(("dp", "expert"), None),
            P(("dp", "expert"), None),
            P(("dp", "expert"), None),
            P(("dp", "expert")),
            P("dp", None),
            P("expert", None, None),
            P("expert", None, None),
            P(),
            P(("dp", "expert"), None),
            P(("dp", "expert"), None),
            P("expert", None, None),
            P("expert", None, None),
            P("expert", None, None),
        ),
        out_specs=P(("dp", "expert"), None),
        check_vma=False,
    )
```

```python
import functools

import jax
import jax.numpy as jnp
from jax import lax
from jax.experimental import pallas as pl
from jax.experimental.pallas import tpu as pltpu
from jax.sharding import PartitionSpec as P

HEAD = 64
GROUPS = 3
BF16, F32 = jnp.bfloat16, jnp.float32
VMEM = pl.BlockSpec(memory_space=pltpu.VMEM)
SMEM = pl.BlockSpec(memory_space=pltpu.SMEM)
ANY = pl.BlockSpec(memory_space=pl.ANY)
MIB = 2**20


def call(kernel, name, out_shape, in_specs, out_specs, scratch, room, flops, **more):
    return pl.pallas_call(
        kernel,
        name=name,
        out_shape=out_shape,
        in_specs=in_specs,
        out_specs=out_specs,
        scratch_shapes=scratch,
        compiler_params=pltpu.CompilerParams(vmem_limit_bytes=room * MIB),
        cost_estimate=pl.CostEstimate(flops=flops, bytes_accessed=1024, transcendentals=0),
        **more,
    )


def attend_kernel(lengths_ref, q_ref, k_ref, v_ref, *refs):
    o_ref, bias = refs[-2:]
    tokens = q_ref.shape[0]
    half = tokens // 2

    @pl.when(pl.program_id(0) == 0)
    def _():
        row = lax.broadcasted_iota(jnp.int32, (tokens, tokens), 0)
        col = lax.broadcasted_iota(jnp.int32, (tokens, tokens), 1)
        same = row >= col
        end = 0
        for r in range(lengths_ref.shape[1]):
            end = end + lengths_ref[0, r]
            same = same & ((row < end) | (col >= end))
        bias[...] = jnp.where(same, 0.0, -1e30)

    for j in range(k_ref.shape[1] // HEAD):
        keys = k_ref[:, j * HEAD : (j + 1) * HEAD]
        values = v_ref[:, j * HEAD : (j + 1) * HEAD]
        for g in range(GROUPS):
            at = (j * GROUPS + g) * HEAD
            q = q_ref[:, at : at + HEAD] * jnp.asarray(HEAD**-0.5, BF16)
            for first, seen in ((0, half), (half, tokens)):
                s = lax.dot_general(
                    q[first : first + half],
                    keys[:seen],
                    (((1,), (1,)), ((), ())),
                    preferred_element_type=F32,
                )
                s = s + bias[first : first + half, :seen]
                p = jnp.exp(s - jnp.max(s, axis=-1, keepdims=True))
                w = (p * (1.0 / jnp.sum(p, axis=-1, keepdims=True))).astype(BF16)
                o = jnp.dot(w, values[:seen], preferred_element_type=F32)
                o_ref[first : first + half, at : at + HEAD] = o.astype(BF16)


def attend(lengths, q, k, v, first, pairs, so_far=None):
    tokens = q.shape[0]
    wide = 2 * GROUPS * HEAD
    return pl.pallas_call(
        attend_kernel,
        name="attend",
        grid=(pairs,),
        out_shape=jax.ShapeDtypeStruct(q.shape, BF16),
        in_specs=[
            SMEM,
            pl.BlockSpec((tokens, wide), lambda i: (0, first + i)),
            pl.BlockSpec((tokens, 2 * HEAD), lambda i: (0, first + i)),
            pl.BlockSpec((tokens, 2 * HEAD), lambda i: (0, first + i)),
        ]
        + ([ANY] if so_far is not None else []),
        out_specs=pl.BlockSpec((tokens, wide), lambda i: (0, first + i)),
        scratch_shapes=[pltpu.VMEM((tokens, tokens), F32)],
        compiler_params=pltpu.CompilerParams(vmem_limit_bytes=8 * MIB),
        cost_estimate=pl.CostEstimate(flops=10**9, bytes_accessed=1024, transcendentals=0),
        input_output_aliases={4: 0} if so_far is not None else {},
    )(lengths, q, k, v, *([so_far] if so_far is not None else []))


GATES, SPAN = 32, 128


def prepare_kernel(logits_ref, routes_ref, gain_ref):
    top, tokens = logits_ref.shape
    logits = logits_ref[...]
    raised = jnp.exp(logits - jnp.max(logits, axis=0, keepdims=True))
    gates = raised / jnp.sum(raised, axis=0, keepdims=True)
    expert = lax.broadcasted_iota(jnp.int32, (GATES, tokens), 0)
    gain = jnp.zeros((GATES, tokens), F32)
    for j in range(top):
        gain = gain + jnp.where(expert == routes_ref[j : j + 1], gates[j : j + 1], 0.0)
    high = gain.astype(BF16).astype(F32)
    rest = jnp.zeros((SPAN - 2 * GATES, tokens), F32)
    gain_ref[...] = jnp.concatenate([high, gain - high, rest], axis=0).T.astype(BF16)


def prepare(logits, routes):
    return call(
        prepare_kernel,
        "prepare",
        jax.ShapeDtypeStruct((logits.shape[1], SPAN), BF16),
        [VMEM] * 2,
        VMEM,
        [],
        4,
        10**9,
    )(logits, routes)


def project_kernel(owners, sources, rank, held, *refs):
    pools, shards = len(owners), len(sources)
    ids, lengths, ctx_ref, res_ref = refs[:4]
    pool, shard = refs[4 : 4 + pools], refs[4 + pools : 4 + pools + shards]
    part_ref, low_s, up_s, sem = refs[-4:]
    requests = ids.shape[0]
    z, i = lax.axis_index("dp"), lax.axis_index("expert")

    def copies(r, ref, first):
        return [
            pltpu.make_async_copy(
                ref.at[pl.ds(first + h * rank, rank)], to.at[pl.ds(r * rank, rank)], sem.at[r, h]
            )
            for h, to in ((0, low_s), (1, up_s))
        ]

    for r in range(requests):
        for k in range(pools):
            at = ids[r] - owners[k](i) * held

            @pl.when((at >= 0) & (at < pool[k].shape[0] // (2 * rank)))
            def _():
                for c in copies(r, pool[k], pl.multiple_of(at * (2 * rank), 2 * rank)):
                    c.start()

    part_ref[...] = res_ref[...].astype(F32)
    for source, piece in zip(sources, shard):
        add_shard(source(z, i), ctx_ref, piece, part_ref)
    for r in range(requests):
        for c in copies(r, pool[0], 0):
            c.wait()
    low = lax.dot_general(
        ctx_ref[...], low_s[...], (((1,), (1,)), ((), ())), preferred_element_type=F32
    )
    row = lax.broadcasted_iota(jnp.int32, low.shape, 0)
    lane = lax.broadcasted_iota(jnp.int32, low.shape, 1)
    end = 0
    mine = lane < 0
    for r in range(requests):
        start, end = end, end + lengths[0, r]
        inside = (row >= start) & (row < end)
        mine = mine | (inside & (lane >= r * rank) & (lane < (r + 1) * rank))
    low = jnp.where(mine, low, 0.0).astype(BF16)
    part_ref[...] += jnp.dot(low, up_s[...], preferred_element_type=F32)


def add_shard(at, ctx_ref, piece, total_ref):
    @pl.when(at >= 0)
    def _():
        first = pl.multiple_of(at, 128)
        total_ref[...] += jnp.dot(
            ctx_ref[:, pl.ds(first, piece.shape[0])], piece[...], preferred_element_type=F32
        )


def project(known, ctx, residual, pools, owners, shards, sources, rank, held):
    requests = known[0].shape[0]
    tokens, width = residual.shape
    return call(
        functools.partial(project_kernel, owners, sources, rank, held),
        "project",
        jax.ShapeDtypeStruct((tokens, width), F32),
        [SMEM] * 2 + [VMEM] * 2 + [ANY] * len(pools) + [VMEM] * len(shards),
        VMEM,
        [
            pltpu.VMEM((requests * rank, width), BF16),
            pltpu.VMEM((requests * rank, width), BF16),
            pltpu.SemaphoreType.DMA((requests, 2)),
        ],
        8,
        10**9,
    )(*known, ctx, residual, *pools, *shards)


def first_columns(width):
    return max(128, width // 384 * 128)


def close_kernel(sources, column, second, *refs):
    part_ref, ctx_ref, scale_ref = refs[:3]
    shard = refs[3 : 3 + len(sources)]
    hidden_ref, send_ref = refs[-2:]
    tokens, width = hidden_ref.shape
    z, i = lax.axis_index("dp"), lax.axis_index("expert")
    hidden_ref[...] = part_ref[:, column : column + width]
    beside = 0
    for source, piece in zip(sources, shard):
        wide = piece.shape[1]
        add_shard(source(z, i), ctx_ref, piece, hidden_ref.at[:, beside : beside + wide])
        beside = (beside + wide) % width
    h = hidden_ref[...]
    scale = scale_ref[...].reshape(1, -1)[:, column : column + width]
    send_ref[:, :width] = (h * scale).astype(BF16)
    if second:
        left_ref, gain_ref = refs[3 + len(sources) : -2]
        left = left_ref[...]
        square = jnp.sum(h * h, axis=-1, keepdims=True)
        square = square + jnp.sum(left * left, axis=-1, keepdims=True)
        inv = lax.rsqrt(square * (1.0 / ctx_ref.shape[1]) + 1e-06)
        high = inv.astype(BF16).astype(F32)
        lane = lax.broadcasted_iota(jnp.int32, (tokens, SPAN), 1)
        gain = gain_ref[...].astype(F32)
        gain = jnp.where(lane == 2 * GATES, high, gain)
        gain = jnp.where(lane == 2 * GATES + 1, inv - high, gain)
        send_ref[:, width:] = gain.astype(BF16)


def close(part, ctx, scale, shards, sources, left=()):
    tokens, width = part.shape
    second = len(left) > 0
    cut = first_columns(width)
    mine = width - cut if second else cut
    return call(
        functools.partial(close_kernel, sources, cut if second else 0, second),
        "close",
        (
            jax.ShapeDtypeStruct((tokens, mine), F32),
            jax.ShapeDtypeStruct((tokens, mine + SPAN if second else mine), BF16),
        ),
        [VMEM] * (3 + len(shards) + len(left)),
        (VMEM, VMEM),
        [],
        8,
        10**9,
    )(part, ctx, scale, *shards, *left)


def experts_kernel(groups, spread, a_ref, b_ref, *refs):
    w, out_ref = refs[: 3 * groups], refs[3 * groups]
    total_ref, x_ref = refs[3 * groups + 1 :]
    local = w[0].shape[0]
    cut, wide = a_ref.shape[1], b_ref.shape[1] - SPAN
    i = lax.axis_index("expert")
    x_ref[:, :cut] = a_ref[...]
    x_ref[:, cut:] = b_ref[:, :wide]
    strip = b_ref[:, wide:].astype(F32)
    lane = lax.broadcasted_iota(jnp.int32, strip.shape, 1)
    inv = strip[:, 2 * GATES : 2 * GATES + 1] + strip[:, 2 * GATES + 1 : 2 * GATES + 2]
    for e in range(groups * local):
        g, own = divmod(e, local)
        number = spread(i, g) * local + own
        mine = (lane == number) | (lane == number + GATES)
        coef = jnp.sum(jnp.where(mine, strip, 0.0), axis=-1, keepdims=True)
        gate = jnp.dot(x_ref[...], w[3 * g][own], preferred_element_type=F32) * inv
        up = jnp.dot(x_ref[...], w[3 * g + 1][own], preferred_element_type=F32)
        act = (gate / (1.0 + jnp.exp(-gate)) * (up * (inv * coef))).astype(BF16)
        down = jnp.dot(act, w[3 * g + 2][own], preferred_element_type=F32)
        if e == 0:
            total_ref[...] = down
        elif e < groups * local - 1:
            total_ref[...] += down
        else:
            out_ref[...] = (total_ref[...] + down).astype(BF16)


def run_experts(x, weights, spread):
    a, b = x
    groups = len(weights) // 3
    tokens, width = a.shape[0], weights[0].shape[1]
    return call(
        functools.partial(experts_kernel, groups, spread),
        "experts",
        jax.ShapeDtypeStruct((tokens, width), BF16),
        [VMEM] * (2 + 3 * groups),
        VMEM,
        [pltpu.VMEM((tokens, width), F32), pltpu.VMEM((tokens, width), BF16)],
        12,
        10**9,
    )(a, b, *weights)


def finish_kernel(left_ref, right_ref, *refs):
    parts, out_ref = refs[:-1], refs[-1]
    at = 0
    for hidden in (left_ref, right_ref):
        to = at + hidden.shape[1]
        total = hidden[...]
        for p in parts:
            total = total + p[:, at:to].astype(F32)
        out_ref[:, at:to] = total.astype(BF16)
        at = to


def finish(left, right, parts):
    return call(
        finish_kernel,
        "finish",
        jax.ShapeDtypeStruct(parts[0].shape, BF16),
        [VMEM] * (2 + len(parts)),
        VMEM,
        [],
        8,
        10**9,
    )(left, right, *parts)


def per_device(
    queries,
    rotated_key_heads,
    token_value_heads,
    residual,
    lengths,
    request_adapter_index,
    attention_output_weight,
    adapter_down_factor,
    adapter_up_factor,
    expert_norm_scale,
    router_logit_scores,
    routes,
    expert_gate_weight,
    expert_up_weight,
    expert_down_weight,
):
    tokens = queries.shape[0]
    rank = adapter_up_factor.shape[1]
    held = adapter_up_factor.shape[0]
    n_dp, n_ex = lax.axis_size("dp"), lax.axis_size("expert")
    rows, width = attention_output_weight.shape
    cut = first_columns(width)
    down_t = jnp.swapaxes(adapter_down_factor, 1, 2)
    weights = (expert_gate_weight, expert_up_weight, expert_down_weight)
    pairs = rotated_key_heads.shape[1] // (2 * HEAD)
    known = (request_adapter_index, lengths)
    own = jnp.concatenate([down_t, adapter_up_factor], axis=1).reshape(-1, width)
    gains = prepare(router_logit_scores.T, routes.T)

    if n_ex != 8 or n_dp != 4:
        context = attend(lengths, queries, rotated_key_heads, token_value_heads, 0, pairs)
        shard = lax.all_gather(attention_output_weight, "dp", axis=0, tiled=True)
        pool = lax.all_gather(own, "expert", axis=0, tiled=True)
        part = project(
            known,
            context,
            residual,
            [pool],
            [lambda i: 0],
            [shard],
            [lambda z, i: z * 0],
            rank,
            held,
        )
        hidden0, send0 = close(part, context, expert_norm_scale, [], [])
        hidden1, send1 = close(part, context, expert_norm_scale, [], [], (hidden0, gains))
        every0 = lax.all_gather(send0, "expert", axis=0, tiled=True)
        every1 = lax.all_gather(send1, "expert", axis=0, tiled=True)
        parts = []
        for d in range(n_ex):
            of = slice(d * tokens, (d + 1) * tokens)
            parts.append(run_experts((every0[of], every1[of]), weights, lambda i, g: i))
        mixture = lax.psum_scatter(
            jnp.concatenate(parts, axis=0), "expert", scatter_dimension=0, tiled=True
        )
        return finish(hidden0, hidden1, [mixture])

    def beside(a):
        return lax.ppermute(a, "expert", [(e, e ^ 1) for e in range(n_ex)])

    def across(a):
        return lax.ppermute(a, "expert", [(e, e ^ (4 if e & 1 else 2)) for e in range(n_ex)])

    def along(a, step):
        sent = []
        for e in range(n_ex):
            for d in range(n_dp):
                to = d - 1 if e & 1 else d + 1
                origin = d + step - 1 if e & 1 else d - step + 1
                if 0 <= to < n_dp and 0 <= origin < n_dp:
                    sent.append((d * n_ex + e, to * n_ex + e))
        return lax.ppermute(a, ("dp", "expert"), sent)

    def after(a, *others):
        return lax.optimization_barrier((a, *others))[0]

    def first_row(step, side):
        def at(z, i):
            source = z + side * step * (1 - 2 * (i & 1))
            return jnp.where((source >= 0) & (source < n_dp), source * rows, -1)

        return at

    def attend_next(first, so_far, *others):
        q = after(queries, *others)
        return attend(lengths, q, rotated_key_heads, token_value_heads, first, 1, so_far)

    z1 = along(attention_output_weight, 1)
    pair_weights = [beside(w) for w in weights[:2]]
    p0 = across(own)
    other = beside(own)
    p1 = across(other)
    context = attend_next(0, None, pair_weights[0])
    z2 = along(after(z1, context), 2)
    context = attend_next(1, context, pair_weights[1])
    p0_other = beside(after(p0, context))
    pair_weights.append(beside(weights[2]))
    context = attend_next(2, context)
    context = attend_next(3, context)
    p2 = across(after(p0_other, p1, context))
    p1_other, p2_other = beside(p1), beside(p2)
    z1_other, z2_other = beside(z1), beside(z2)
    z3 = [along(z2[:, :cut], 3), along(z2[:, cut:], 3)]
    owners = [
        lambda i: i,
        lambda i: i ^ 1,
        lambda i: i ^ (2 + 2 * (i & 1)),
        lambda i: i ^ (3 + 2 * (i & 1)),
        lambda i: i ^ (5 - 2 * (i & 1)),
        lambda i: i ^ (4 - 2 * (i & 1)),
        lambda i: i ^ 7,
        lambda i: i ^ 6,
    ]
    part = project(
        known,
        context,
        after(residual, pair_weights[2]),
        [own, other, p0, p1, p0_other, p1_other, p2, p2_other],
        owners,
        [attention_output_weight, z1, z1_other, z2, z2_other],
        [lambda z, i: z * rows] + [first_row(s, side) for s in (1, 2) for side in (-1, 1)],
        rank,
        held,
    )
    ends = [first_row(3, -1), first_row(3, 1)]
    task = functools.partial(close, part, context, expert_norm_scale)
    hidden0, send0 = task([z3[0], beside(after(z3[0], part))], ends)
    other0 = beside(send0)
    near0, next0 = across(send0), across(other0)
    late = after(z3[1], send0)
    parts = [z3[1], beside(late[:, :cut]), beside(late[:, cut:])]
    hidden1, send1 = task(parts, [ends[0], ends[1], ends[1]], (hidden0, gains))
    near0_other = beside(near0)
    far0 = across(near0_other)
    other1 = beside(send1)
    near1, next1 = across(after(send1, near0_other)), across(other1)
    run = functools.partial(
        run_experts, weights=weights + tuple(pair_weights), spread=lambda i, g: i ^ g
    )
    home = run((send0, send1))
    far1 = across(beside(after(near1, next0, home)))
    r_near = run((near0, after(near1, home)))
    r_next = run((next0, after(next1, r_near)))
    back = across(r_next)
    r_far = run((far0, after(far1, r_next)))
    via = beside(after(across(r_far), back))
    back1 = beside(back)
    back0 = across((r_near.astype(F32) + via.astype(F32)).astype(BF16))
    return finish(hidden0, hidden1, [home, back1, back0])


def solution(mesh):
    return jax.shard_map(
        per_device,
        mesh=mesh,
        in_specs=(
            P(("dp", "expert"), None),
            P(("dp", "expert"), None),
            P(("dp", "expert"), None),
            P(("dp", "expert"), None),
            P(("dp", "expert"), None),
            P(("dp", "expert")),
            P("dp", None),
            P("expert", None, None),
            P("expert", None, None),
            P(),
            P(("dp", "expert"), None),
            P(("dp", "expert"), None),
            P("expert", None, None),
            P("expert", None, None),
            P("expert", None, None),
        ),
        out_specs=P(("dp", "expert"), None),
        check_vma=False,
    )
```

```python
import functools

import jax
import jax.numpy as jnp
from jax import lax
from jax.experimental import pallas as pl
from jax.experimental.pallas import tpu as pltpu
from jax.sharding import PartitionSpec as P

HEAD = 64
GROUPS = 3
BF16, F32 = jnp.bfloat16, jnp.float32
VMEM = pl.BlockSpec(memory_space=pltpu.VMEM)
SMEM = pl.BlockSpec(memory_space=pltpu.SMEM)
ANY = pl.BlockSpec(memory_space=pl.ANY)
MIB = 2**20


def call(kernel, name, out_shape, in_specs, out_specs, scratch, room, flops, **more):
    return pl.pallas_call(
        kernel,
        name=name,
        out_shape=out_shape,
        in_specs=in_specs,
        out_specs=out_specs,
        scratch_shapes=scratch,
        compiler_params=pltpu.CompilerParams(vmem_limit_bytes=room * MIB),
        cost_estimate=pl.CostEstimate(flops=flops, bytes_accessed=1024, transcendentals=0),
        **more,
    )


def attend_kernel(lengths_ref, q_ref, k_ref, v_ref, *refs):
    o_ref, bias = refs[-2:]
    tokens = q_ref.shape[0]
    half = tokens // 2

    @pl.when(pl.program_id(0) == 0)
    def _():
        row = lax.broadcasted_iota(jnp.int32, (tokens, tokens), 0)
        col = lax.broadcasted_iota(jnp.int32, (tokens, tokens), 1)
        same = row >= col
        end = 0
        for r in range(lengths_ref.shape[1]):
            end = end + lengths_ref[0, r]
            same = same & ((row < end) | (col >= end))
        bias[...] = jnp.where(same, 0.0, -1e30)

    for j in range(k_ref.shape[1] // HEAD):
        keys = k_ref[:, j * HEAD : (j + 1) * HEAD]
        values = v_ref[:, j * HEAD : (j + 1) * HEAD]
        for g in range(GROUPS):
            at = (j * GROUPS + g) * HEAD
            q = q_ref[:, at : at + HEAD] * jnp.asarray(HEAD**-0.5, BF16)
            for first, seen in ((0, half), (half, tokens)):
                s = lax.dot_general(
                    q[first : first + half],
                    keys[:seen],
                    (((1,), (1,)), ((), ())),
                    preferred_element_type=F32,
                )
                s = s + bias[first : first + half, :seen]
                p = jnp.exp(s - jnp.max(s, axis=-1, keepdims=True))
                w = (p * (1.0 / jnp.sum(p, axis=-1, keepdims=True))).astype(BF16)
                o = jnp.dot(w, values[:seen], preferred_element_type=F32)
                o_ref[first : first + half, at : at + HEAD] = o.astype(BF16)


def attend(lengths, q, k, v, first, pairs, so_far=None):
    tokens = q.shape[0]
    wide = 2 * GROUPS * HEAD
    return pl.pallas_call(
        attend_kernel,
        name="attend",
        grid=(pairs,),
        out_shape=jax.ShapeDtypeStruct(q.shape, BF16),
        in_specs=[
            SMEM,
            pl.BlockSpec((tokens, wide), lambda i: (0, first + i)),
            pl.BlockSpec((tokens, 2 * HEAD), lambda i: (0, first + i)),
            pl.BlockSpec((tokens, 2 * HEAD), lambda i: (0, first + i)),
        ]
        + ([ANY] if so_far is not None else []),
        out_specs=pl.BlockSpec((tokens, wide), lambda i: (0, first + i)),
        scratch_shapes=[pltpu.VMEM((tokens, tokens), F32)],
        compiler_params=pltpu.CompilerParams(vmem_limit_bytes=8 * MIB),
        cost_estimate=pl.CostEstimate(flops=10**9, bytes_accessed=1024, transcendentals=0),
        input_output_aliases={4: 0} if so_far is not None else {},
    )(lengths, q, k, v, *([so_far] if so_far is not None else []))


GATES, SPAN = 32, 128


def prepare_kernel(logits_ref, routes_ref, gain_ref):
    top, tokens = logits_ref.shape
    logits = logits_ref[...]
    raised = jnp.exp(logits - jnp.max(logits, axis=0, keepdims=True))
    gates = raised / jnp.sum(raised, axis=0, keepdims=True)
    expert = lax.broadcasted_iota(jnp.int32, (GATES, tokens), 0)
    gain = jnp.zeros((GATES, tokens), F32)
    for j in range(top):
        gain = gain + jnp.where(expert == routes_ref[j : j + 1], gates[j : j + 1], 0.0)
    high = gain.astype(BF16).astype(F32)
    rest = jnp.zeros((SPAN - 2 * GATES, tokens), F32)
    gain_ref[...] = jnp.concatenate([high, gain - high, rest], axis=0).T.astype(BF16)


def prepare(logits, routes):
    return call(
        prepare_kernel,
        "prepare",
        jax.ShapeDtypeStruct((logits.shape[1], SPAN), BF16),
        [VMEM] * 2,
        VMEM,
        [],
        4,
        10**9,
    )(logits, routes)


def project_kernel(sources, ctx_ref, res_ref, *refs):
    shard, part_ref = refs[:-1], refs[-1]
    z, i = lax.axis_index("dp"), lax.axis_index("expert")
    part_ref[...] = res_ref[...].astype(F32)
    for source, piece in zip(sources, shard):
        add_shard(source(z, i), ctx_ref, piece, part_ref)


def adapt_kernel(owners, rank, *refs):
    ids, lengths, ctx_ref, part_ref = refs[:4]
    pool = refs[4:-4]
    out_ref, low_s, up_s, sem = refs[-4:]
    requests = ids.shape[0]
    i = lax.axis_index("expert")

    def copies(r, ref, first):
        return [
            pltpu.make_async_copy(
                ref.at[pl.ds(first + h * rank, rank)], to.at[pl.ds(r * rank, rank)], sem.at[r, h]
            )
            for h, to in ((0, low_s), (1, up_s))
        ]

    for r in range(requests):
        for k, owner in enumerate(owners):
            at = ids[r] - owner(i)

            @pl.when((at >= 0) & (at < pool[k].shape[0] // (2 * rank)))
            def _():
                for c in copies(r, pool[k], pl.multiple_of(at * (2 * rank), 2 * rank)):
                    c.start()

    for r in range(requests):
        for c in copies(r, pool[0], 0):
            c.wait()
    low = lax.dot_general(
        ctx_ref[...], low_s[...], (((1,), (1,)), ((), ())), preferred_element_type=F32
    )
    row = lax.broadcasted_iota(jnp.int32, low.shape, 0)
    lane = lax.broadcasted_iota(jnp.int32, low.shape, 1)
    end = 0
    mine = lane < 0
    for r in range(requests):
        start, end = end, end + lengths[0, r]
        inside = (row >= start) & (row < end)
        mine = mine | (inside & (lane >= r * rank) & (lane < (r + 1) * rank))
    low = jnp.where(mine, low, 0.0).astype(BF16)
    out_ref[...] = part_ref[...] + jnp.dot(low, up_s[...], preferred_element_type=F32)


def add_shard(at, ctx_ref, piece, total_ref):
    @pl.when(at >= 0)
    def _():
        first = pl.multiple_of(at, 128)
        total_ref[...] += jnp.dot(
            ctx_ref[:, pl.ds(first, piece.shape[0])], piece[...], preferred_element_type=F32
        )


def project(ctx, residual, shards, sources):
    return call(
        functools.partial(project_kernel, sources),
        "project",
        jax.ShapeDtypeStruct(residual.shape, F32),
        [VMEM] * (2 + len(shards)),
        VMEM,
        [],
        8,
        10**9,
    )(ctx, residual, *shards)


def adapt(known, ctx, part, pools, owners, rank):
    requests, width = known[0].shape[0], part.shape[1]
    return call(
        functools.partial(adapt_kernel, owners, rank),
        "adapt",
        jax.ShapeDtypeStruct(part.shape, F32),
        [SMEM] * 2 + [VMEM] * 2 + [ANY] * len(pools),
        VMEM,
        [
            pltpu.VMEM((requests * rank, width), BF16),
            pltpu.VMEM((requests * rank, width), BF16),
            pltpu.SemaphoreType.DMA((requests, 2)),
        ],
        8,
        10**9,
    )(*known, ctx, part, *pools)


def first_columns(width):
    return max(128, width // 384 * 128)


def close_kernel(sources, column, second, *refs):
    part_ref, ctx_ref, scale_ref = refs[:3]
    shard = refs[3 : 3 + len(sources)]
    hidden_ref, send_ref = refs[-2:]
    tokens, width = hidden_ref.shape
    z, i = lax.axis_index("dp"), lax.axis_index("expert")
    hidden_ref[...] = part_ref[:, column : column + width]
    beside = 0
    for source, piece in zip(sources, shard):
        wide = piece.shape[1]
        add_shard(source(z, i), ctx_ref, piece, hidden_ref.at[:, beside : beside + wide])
        beside = (beside + wide) % width
    h = hidden_ref[...]
    scale = scale_ref[...].reshape(1, -1)[:, column : column + width]
    send_ref[:, :width] = (h * scale).astype(BF16)
    if second:
        left_ref, gain_ref = refs[3 + len(sources) : -2]
        left = left_ref[...]
        square = jnp.sum(h * h, axis=-1, keepdims=True)
        square = square + jnp.sum(left * left, axis=-1, keepdims=True)
        inv = lax.rsqrt(square * (1.0 / ctx_ref.shape[1]) + 1e-06)
        high = inv.astype(BF16).astype(F32)
        lane = lax.broadcasted_iota(jnp.int32, (tokens, SPAN), 1)
        gain = gain_ref[...].astype(F32)
        gain = jnp.where(lane == 2 * GATES, high, gain)
        gain = jnp.where(lane == 2 * GATES + 1, inv - high, gain)
        send_ref[:, width:] = gain.astype(BF16)


def close(part, ctx, scale, shards, sources, left=()):
    tokens, width = part.shape
    second = len(left) > 0
    cut = first_columns(width)
    mine = width - cut if second else cut
    return call(
        functools.partial(close_kernel, sources, cut if second else 0, second),
        "close",
        (
            jax.ShapeDtypeStruct((tokens, mine), F32),
            jax.ShapeDtypeStruct((tokens, mine + SPAN if second else mine), BF16),
        ),
        [VMEM] * (3 + len(shards) + len(left)),
        (VMEM, VMEM),
        [],
        8,
        10**9,
    )(part, ctx, scale, *shards, *left)


def experts_kernel(groups, spread, a_ref, b_ref, *refs):
    w, out_ref = refs[: 3 * groups], refs[3 * groups]
    total_ref, x_ref = refs[3 * groups + 1 :]
    local = w[0].shape[0]
    cut, wide = a_ref.shape[1], b_ref.shape[1] - SPAN
    i = lax.axis_index("expert")
    x_ref[:, :cut] = a_ref[...]
    x_ref[:, cut:] = b_ref[:, :wide]
    strip = b_ref[:, wide:].astype(F32)
    lane = lax.broadcasted_iota(jnp.int32, strip.shape, 1)
    inv = strip[:, 2 * GATES : 2 * GATES + 1] + strip[:, 2 * GATES + 1 : 2 * GATES + 2]
    for e in range(groups * local):
        g, own = divmod(e, local)
        number = spread(i, g) * local + own
        mine = (lane == number) | (lane == number + GATES)
        coef = jnp.sum(jnp.where(mine, strip, 0.0), axis=-1, keepdims=True)
        gate = jnp.dot(x_ref[...], w[3 * g][own], preferred_element_type=F32) * inv
        up = jnp.dot(x_ref[...], w[3 * g + 1][own], preferred_element_type=F32)
        act = (gate / (1.0 + jnp.exp(-gate)) * (up * (inv * coef))).astype(BF16)
        down = jnp.dot(act, w[3 * g + 2][own], preferred_element_type=F32)
        if e == 0:
            total_ref[...] = down
        elif e < groups * local - 1:
            total_ref[...] += down
        else:
            out_ref[...] = (total_ref[...] + down).astype(BF16)


def run_experts(x, weights, spread):
    a, b = x
    groups = len(weights) // 3
    tokens, width = a.shape[0], weights[0].shape[1]
    return call(
        functools.partial(experts_kernel, groups, spread),
        "experts",
        jax.ShapeDtypeStruct((tokens, width), BF16),
        [VMEM] * (2 + 3 * groups),
        VMEM,
        [pltpu.VMEM((tokens, width), F32), pltpu.VMEM((tokens, width), BF16)],
        12,
        10**9,
    )(a, b, *weights)


def finish_kernel(left_ref, right_ref, *refs):
    parts, out_ref = refs[:-1], refs[-1]
    at = 0
    for hidden in (left_ref, right_ref):
        to = at + hidden.shape[1]
        total = hidden[...]
        for p in parts:
            total = total + p[:, at:to].astype(F32)
        out_ref[:, at:to] = total.astype(BF16)
        at = to


def finish(left, right, parts):
    return call(
        finish_kernel,
        "finish",
        jax.ShapeDtypeStruct(parts[0].shape, BF16),
        [VMEM] * (2 + len(parts)),
        VMEM,
        [],
        8,
        10**9,
    )(left, right, *parts)


def per_device(
    queries,
    rotated_key_heads,
    token_value_heads,
    residual,
    lengths,
    request_adapter_index,
    attention_output_weight,
    adapter_down_factor,
    adapter_up_factor,
    expert_norm_scale,
    router_logit_scores,
    routes,
    expert_gate_weight,
    expert_up_weight,
    expert_down_weight,
):
    tokens = queries.shape[0]
    rank = adapter_up_factor.shape[1]
    held = adapter_up_factor.shape[0]
    n_dp, n_ex = lax.axis_size("dp"), lax.axis_size("expert")
    rows, width = attention_output_weight.shape
    cut = first_columns(width)
    down_t = jnp.swapaxes(adapter_down_factor, 1, 2)
    weights = (expert_gate_weight, expert_up_weight, expert_down_weight)
    pairs = rotated_key_heads.shape[1] // (2 * HEAD)
    known = (request_adapter_index, lengths)
    own = jnp.concatenate([down_t, adapter_up_factor], axis=1).reshape(-1, width)
    gains = prepare(router_logit_scores.T, routes.T)

    if n_ex != 8 or n_dp != 4:
        context = attend(lengths, queries, rotated_key_heads, token_value_heads, 0, pairs)
        shard = lax.all_gather(attention_output_weight, "dp", axis=0, tiled=True)
        pool = lax.all_gather(own, "expert", axis=0, tiled=True)
        part = project(context, residual, [shard], [lambda z, i: z * 0])
        part = adapt(known, context, part, [pool], [lambda i: i * 0], rank)
        hidden0, send0 = close(part, context, expert_norm_scale, [], [])
        hidden1, send1 = close(part, context, expert_norm_scale, [], [], (hidden0, gains))
        every0 = lax.all_gather(send0, "expert", axis=0, tiled=True)
        every1 = lax.all_gather(send1, "expert", axis=0, tiled=True)
        parts = []
        for d in range(n_ex):
            of = slice(d * tokens, (d + 1) * tokens)
            parts.append(run_experts((every0[of], every1[of]), weights, lambda i, g: i))
        mixture = lax.psum_scatter(
            jnp.concatenate(parts, axis=0), "expert", scatter_dimension=0, tiled=True
        )
        return finish(hidden0, hidden1, [mixture])

    def beside(a):
        return lax.ppermute(a, "expert", [(e, e ^ 1) for e in range(n_ex)])

    def across(a):
        return lax.ppermute(a, "expert", [(e, e ^ (4 if e & 1 else 2)) for e in range(n_ex)])

    def turned(a):
        return lax.ppermute(a, "expert", [(e, e ^ (3 if e & 1 else 5)) for e in range(n_ex)])

    def along(a, step):
        sent = []
        for e in range(n_ex):
            for d in range(n_dp):
                to = d - 1 if e & 1 else d + 1
                origin = d + step - 1 if e & 1 else d - step + 1
                if 0 <= to < n_dp and 0 <= origin < n_dp:
                    sent.append((d * n_ex + e, to * n_ex + e))
        return lax.ppermute(a, ("dp", "expert"), sent)

    def after(a, *others):
        return lax.optimization_barrier((a, *others))[0]

    def first_row(step, side):
        def at(z, i):
            source = z + side * step * (1 - 2 * (i & 1))
            return jnp.where((source >= 0) & (source < n_dp), source * rows, -1)

        return at

    def attend_next(first, so_far, *others):
        q = after(queries, *others)
        return attend(lengths, q, rotated_key_heads, token_value_heads, first, 1, so_far)

    z1 = along(attention_output_weight, 1)
    pair_weights = [beside(w) for w in weights[:2]]
    p0 = across(own)
    other = beside(own)
    p1 = across(other)
    context = attend_next(0, None, pair_weights[0])
    z2 = along(after(z1, context), 2)
    p0_other = beside(after(p0, context))
    context = attend_next(1, context, pair_weights[1])
    pair_weights.append(beside(weights[2]))
    context = attend_next(2, context, pair_weights[2])
    context = attend_next(3, context)
    p2 = across(after(p0_other, p1, context))
    p1_other = beside(p1)
    z1_other, z2_other = beside(z1), beside(z2)
    z3 = [along(z2[:, :cut], 3), along(z2[:, cut:], 3)]
    few = held * 3 // 4
    owners = [
        lambda i: i * held,
        lambda i: (i ^ 1) * held,
        lambda i: (i ^ (2 + 2 * (i & 1))) * held,
        lambda i: (i ^ (3 + 2 * (i & 1))) * held,
        lambda i: (i ^ (5 - 2 * (i & 1))) * held,
        lambda i: (i ^ (4 - 2 * (i & 1))) * held,
        lambda i: (i ^ 7) * held,
        lambda i: (i ^ 6) * held,
        lambda i: (i ^ 6) * held + few,
    ]
    part = project(
        context,
        residual,
        [attention_output_weight, z1, z1_other, z2, z2_other],
        [lambda z, i: z * rows] + [first_row(s, side) for s in (1, 2) for side in (-1, 1)],
    )
    p2_other = [beside(p2[: few * 2 * rank]), beside(p2[few * 2 * rank :])]
    pools = [own, other, p0, p1, p0_other, p1_other, p2, *p2_other]
    whole = adapt(known, context, part, pools, owners, rank)
    ends = [first_row(3, -1), first_row(3, 1)]
    task = functools.partial(close, whole, context, expert_norm_scale)
    hidden0, send0 = task([z3[0], beside(z3[0])], ends)
    other0 = beside(send0)
    near0, next0 = across(send0), across(other0)
    late = after(z3[1], send0)
    parts = [z3[1], beside(late[:, :cut]), beside(late[:, cut:])]
    hidden1, send1 = task(parts, [ends[0], ends[1], ends[1]], (hidden0, gains))
    near0_other = beside(near0)
    far0 = across(near0_other)
    other1 = beside(send1)
    near1, next1 = across(after(send1, near0_other)), across(other1)
    run = functools.partial(
        run_experts, weights=weights + tuple(pair_weights), spread=lambda i, g: i ^ g
    )
    home = run((send0, send1))
    far1 = across(beside(after(near1, next0, home)))
    r_near = run((near0, after(near1, home)))
    r_next = run((next0, after(next1, r_near)))
    back = across(r_next)
    r_far = run((far0, after(far1, r_next)))
    ready = beside(r_near)
    far_sum = across(r_far).astype(F32) + ready.astype(F32)
    back1 = beside(back)
    back0 = turned(far_sum.astype(BF16))
    return finish(hidden0, hidden1, [home, back1, back0])


def solution(mesh):
    return jax.shard_map(
        per_device,
        mesh=mesh,
        in_specs=(
            P(("dp", "expert"), None),
            P(("dp", "expert"), None),
            P(("dp", "expert"), None),
            P(("dp", "expert"), None),
            P(("dp", "expert"), None),
            P(("dp", "expert")),
            P("dp", None),
            P("expert", None, None),
            P("expert", None, None),
            P(),
            P(("dp", "expert"), None),
            P(("dp", "expert"), None),
            P("expert", None, None),
            P("expert", None, None),
            P("expert", None, None),
        ),
        out_specs=P(("dp", "expert"), None),
        check_vma=False,
    )
```

```python
import functools

import jax
import jax.numpy as jnp
from jax import lax
from jax.experimental import pallas as pl
from jax.experimental.pallas import tpu as pltpu
from jax.sharding import PartitionSpec as P

HEAD = 64
GROUPS = 3
BF16, F32 = jnp.bfloat16, jnp.float32
VMEM = pl.BlockSpec(memory_space=pltpu.VMEM)
SMEM = pl.BlockSpec(memory_space=pltpu.SMEM)
ANY = pl.BlockSpec(memory_space=pl.ANY)
MIB = 2**20


def call(kernel, name, out_shape, in_specs, out_specs, scratch, room, flops, **more):
    return pl.pallas_call(
        kernel,
        name=name,
        out_shape=out_shape,
        in_specs=in_specs,
        out_specs=out_specs,
        scratch_shapes=scratch,
        compiler_params=pltpu.CompilerParams(vmem_limit_bytes=room * MIB),
        cost_estimate=pl.CostEstimate(flops=flops, bytes_accessed=1024, transcendentals=0),
        **more,
    )


def attend_kernel(lengths_ref, q_ref, k_ref, v_ref, *refs):
    o_ref, bias = refs[-2:]
    tokens = q_ref.shape[0]
    half = tokens // 2

    @pl.when(pl.program_id(0) == 0)
    def _():
        row = lax.broadcasted_iota(jnp.int32, (tokens, tokens), 0)
        col = lax.broadcasted_iota(jnp.int32, (tokens, tokens), 1)
        same = row >= col
        end = 0
        for r in range(lengths_ref.shape[1]):
            end = end + lengths_ref[0, r]
            same = same & ((row < end) | (col >= end))
        bias[...] = jnp.where(same, 0.0, -1e30)

    for j in range(k_ref.shape[1] // HEAD):
        keys = k_ref[:, j * HEAD : (j + 1) * HEAD]
        values = v_ref[:, j * HEAD : (j + 1) * HEAD]
        for g in range(GROUPS):
            at = (j * GROUPS + g) * HEAD
            q = q_ref[:, at : at + HEAD] * jnp.asarray(HEAD**-0.5, BF16)
            for first, seen in ((0, half), (half, tokens)):
                s = lax.dot_general(
                    q[first : first + half],
                    keys[:seen],
                    (((1,), (1,)), ((), ())),
                    preferred_element_type=F32,
                )
                s = s + bias[first : first + half, :seen]
                p = jnp.exp(s - jnp.max(s, axis=-1, keepdims=True))
                w = (p * (1.0 / jnp.sum(p, axis=-1, keepdims=True))).astype(BF16)
                o = jnp.dot(w, values[:seen], preferred_element_type=F32)
                o_ref[first : first + half, at : at + HEAD] = o.astype(BF16)


def attend(lengths, q, k, v, first, pairs, so_far=None):
    tokens = q.shape[0]
    wide = 2 * GROUPS * HEAD
    return pl.pallas_call(
        attend_kernel,
        name="attend",
        grid=(pairs,),
        out_shape=jax.ShapeDtypeStruct(q.shape, BF16),
        in_specs=[
            SMEM,
            pl.BlockSpec((tokens, wide), lambda i: (0, first + i)),
            pl.BlockSpec((tokens, 2 * HEAD), lambda i: (0, first + i)),
            pl.BlockSpec((tokens, 2 * HEAD), lambda i: (0, first + i)),
        ]
        + ([ANY] if so_far is not None else []),
        out_specs=pl.BlockSpec((tokens, wide), lambda i: (0, first + i)),
        scratch_shapes=[pltpu.VMEM((tokens, tokens), F32)],
        compiler_params=pltpu.CompilerParams(vmem_limit_bytes=8 * MIB),
        cost_estimate=pl.CostEstimate(flops=10**9, bytes_accessed=1024, transcendentals=0),
        input_output_aliases={4: 0} if so_far is not None else {},
    )(lengths, q, k, v, *([so_far] if so_far is not None else []))


GATES, SPAN = 32, 128


def prepare_kernel(logits_ref, routes_ref, gain_ref):
    top, tokens = logits_ref.shape
    logits = logits_ref[...]
    raised = jnp.exp(logits - jnp.max(logits, axis=0, keepdims=True))
    gates = raised / jnp.sum(raised, axis=0, keepdims=True)
    expert = lax.broadcasted_iota(jnp.int32, (GATES, tokens), 0)
    gain = jnp.zeros((GATES, tokens), F32)
    for j in range(top):
        gain = gain + jnp.where(expert == routes_ref[j : j + 1], gates[j : j + 1], 0.0)
    high = gain.astype(BF16).astype(F32)
    rest = jnp.zeros((SPAN - 2 * GATES, tokens), F32)
    gain_ref[...] = jnp.concatenate([high, gain - high, rest], axis=0).T.astype(BF16)


def prepare(logits, routes):
    return call(
        prepare_kernel,
        "prepare",
        jax.ShapeDtypeStruct((logits.shape[1], SPAN), BF16),
        [VMEM] * 2,
        VMEM,
        [],
        4,
        10**9,
    )(logits, routes)


def project_kernel(sources, ctx_ref, res_ref, *refs):
    shard, part_ref = refs[:-1], refs[-1]
    z, i = lax.axis_index("dp"), lax.axis_index("expert")
    part_ref[...] = res_ref[...].astype(F32)
    for source, piece in zip(sources, shard):
        add_shard(source(z, i), ctx_ref, piece, part_ref)


def adapt_kernel(owners, rank, *refs):
    ids, lengths, ctx_ref, part_ref = refs[:4]
    pool = refs[4:-4]
    out_ref, low_s, up_s, sem = refs[-4:]
    requests = ids.shape[0]
    i = lax.axis_index("expert")

    def copies(r, ref, first):
        return [
            pltpu.make_async_copy(
                ref.at[pl.ds(first + h * rank, rank)], to.at[pl.ds(r * rank, rank)], sem.at[r, h]
            )
            for h, to in ((0, low_s), (1, up_s))
        ]

    for r in range(requests):
        for k, owner in enumerate(owners):
            at = ids[r] - owner(i)

            @pl.when((at >= 0) & (at < pool[k].shape[0] // (2 * rank)))
            def _():
                for c in copies(r, pool[k], pl.multiple_of(at * (2 * rank), 2 * rank)):
                    c.start()

    for r in range(requests):
        for c in copies(r, pool[0], 0):
            c.wait()
    low = lax.dot_general(
        ctx_ref[...], low_s[...], (((1,), (1,)), ((), ())), preferred_element_type=F32
    )
    row = lax.broadcasted_iota(jnp.int32, low.shape, 0)
    lane = lax.broadcasted_iota(jnp.int32, low.shape, 1)
    end = 0
    mine = lane < 0
    for r in range(requests):
        start, end = end, end + lengths[0, r]
        inside = (row >= start) & (row < end)
        mine = mine | (inside & (lane >= r * rank) & (lane < (r + 1) * rank))
    low = jnp.where(mine, low, 0.0).astype(BF16)
    out_ref[...] = part_ref[...] + jnp.dot(low, up_s[...], preferred_element_type=F32)


def add_shard(at, ctx_ref, piece, total_ref):
    @pl.when(at >= 0)
    def _():
        first = pl.multiple_of(at, 128)
        total_ref[...] += jnp.dot(
            ctx_ref[:, pl.ds(first, piece.shape[0])], piece[...], preferred_element_type=F32
        )


def project(ctx, residual, shards, sources):
    return call(
        functools.partial(project_kernel, sources),
        "project",
        jax.ShapeDtypeStruct(residual.shape, F32),
        [VMEM] * (2 + len(shards)),
        VMEM,
        [],
        8,
        10**9,
    )(ctx, residual, *shards)


def adapt(known, ctx, part, pools, owners, rank):
    requests, width = known[0].shape[0], part.shape[1]
    return call(
        functools.partial(adapt_kernel, owners, rank),
        "adapt",
        jax.ShapeDtypeStruct(part.shape, F32),
        [SMEM] * 2 + [VMEM] * 2 + [ANY] * len(pools),
        VMEM,
        [
            pltpu.VMEM((requests * rank, width), BF16),
            pltpu.VMEM((requests * rank, width), BF16),
            pltpu.SemaphoreType.DMA((requests, 2)),
        ],
        8,
        10**9,
    )(*known, ctx, part, *pools)


def first_columns(width):
    return max(128, width // 384 * 128)


def close_kernel(sources, column, second, *refs):
    part_ref, ctx_ref, scale_ref = refs[:3]
    shard = refs[3 : 3 + len(sources)]
    hidden_ref, send_ref = refs[-2:]
    tokens, width = hidden_ref.shape
    z, i = lax.axis_index("dp"), lax.axis_index("expert")
    hidden_ref[...] = part_ref[:, column : column + width]
    beside = 0
    for source, piece in zip(sources, shard):
        wide = piece.shape[1]
        add_shard(source(z, i), ctx_ref, piece, hidden_ref.at[:, beside : beside + wide])
        beside = (beside + wide) % width
    h = hidden_ref[...]
    scale = scale_ref[...].reshape(1, -1)[:, column : column + width]
    send_ref[:, :width] = (h * scale).astype(BF16)
    if second:
        left_ref, gain_ref = refs[3 + len(sources) : -2]
        left = left_ref[...]
        square = jnp.sum(h * h, axis=-1, keepdims=True)
        square = square + jnp.sum(left * left, axis=-1, keepdims=True)
        inv = lax.rsqrt(square * (1.0 / ctx_ref.shape[1]) + 1e-06)
        high = inv.astype(BF16).astype(F32)
        lane = lax.broadcasted_iota(jnp.int32, (tokens, SPAN), 1)
        gain = gain_ref[...].astype(F32)
        gain = jnp.where(lane == 2 * GATES, high, gain)
        gain = jnp.where(lane == 2 * GATES + 1, inv - high, gain)
        send_ref[:, width:] = gain.astype(BF16)


def close(part, ctx, scale, shards, sources, left=()):
    tokens, width = part.shape
    second = len(left) > 0
    cut = first_columns(width)
    mine = width - cut if second else cut
    return call(
        functools.partial(close_kernel, sources, cut if second else 0, second),
        "close",
        (
            jax.ShapeDtypeStruct((tokens, mine), F32),
            jax.ShapeDtypeStruct((tokens, mine + SPAN if second else mine), BF16),
        ),
        [VMEM] * (3 + len(shards) + len(left)),
        (VMEM, VMEM),
        [],
        8,
        10**9,
    )(part, ctx, scale, *shards, *left)


def experts_kernel(groups, spread, a_ref, b_ref, *refs):
    w, out_ref = refs[: 3 * groups], refs[3 * groups]
    total_ref, x_ref = refs[3 * groups + 1 :]
    local = w[0].shape[0]
    cut, wide = a_ref.shape[1], b_ref.shape[1] - SPAN
    i = lax.axis_index("expert")
    x_ref[:, :cut] = a_ref[...]
    x_ref[:, cut:] = b_ref[:, :wide]
    strip = b_ref[:, wide:].astype(F32)
    lane = lax.broadcasted_iota(jnp.int32, strip.shape, 1)
    inv = strip[:, 2 * GATES : 2 * GATES + 1] + strip[:, 2 * GATES + 1 : 2 * GATES + 2]
    for e in range(groups * local):
        g, own = divmod(e, local)
        number = spread(i, g) * local + own
        mine = (lane == number) | (lane == number + GATES)
        coef = jnp.sum(jnp.where(mine, strip, 0.0), axis=-1, keepdims=True)
        gate = jnp.dot(x_ref[...], w[3 * g][own], preferred_element_type=F32) * inv
        up = jnp.dot(x_ref[...], w[3 * g + 1][own], preferred_element_type=F32)
        act = (gate / (1.0 + jnp.exp(-gate)) * (up * (inv * coef))).astype(BF16)
        down = jnp.dot(act, w[3 * g + 2][own], preferred_element_type=F32)
        if e == 0:
            total_ref[...] = down
        elif e < groups * local - 1:
            total_ref[...] += down
        else:
            out_ref[...] = (total_ref[...] + down).astype(BF16)


def run_experts(x, weights, spread):
    a, b = x
    groups = len(weights) // 3
    tokens, width = a.shape[0], weights[0].shape[1]
    return call(
        functools.partial(experts_kernel, groups, spread),
        "experts",
        jax.ShapeDtypeStruct((tokens, width), BF16),
        [VMEM] * (2 + 3 * groups),
        VMEM,
        [pltpu.VMEM((tokens, width), F32), pltpu.VMEM((tokens, width), BF16)],
        12,
        10**9,
    )(a, b, *weights)


def finish_kernel(left_ref, right_ref, *refs):
    parts, out_ref = refs[:-1], refs[-1]
    at = 0
    for hidden in (left_ref, right_ref):
        to = at + hidden.shape[1]
        total = hidden[...]
        for p in parts:
            total = total + p[:, at:to].astype(F32)
        out_ref[:, at:to] = total.astype(out_ref.dtype)
        at = to


def finish(left, right, parts, kind=BF16):
    return call(
        finish_kernel,
        "finish",
        jax.ShapeDtypeStruct(parts[0].shape, kind),
        [VMEM] * (2 + len(parts)),
        VMEM,
        [],
        8,
        10**9,
    )(left, right, *parts)


def per_device(
    queries,
    rotated_key_heads,
    token_value_heads,
    residual,
    lengths,
    request_adapter_index,
    attention_output_weight,
    adapter_down_factor,
    adapter_up_factor,
    expert_norm_scale,
    router_logit_scores,
    routes,
    expert_gate_weight,
    expert_up_weight,
    expert_down_weight,
):
    tokens = queries.shape[0]
    rank = adapter_up_factor.shape[1]
    held = adapter_up_factor.shape[0]
    n_dp, n_ex = lax.axis_size("dp"), lax.axis_size("expert")
    rows, width = attention_output_weight.shape
    cut = first_columns(width)
    down_t = jnp.swapaxes(adapter_down_factor, 1, 2)
    weights = (expert_gate_weight, expert_up_weight, expert_down_weight)
    pairs = rotated_key_heads.shape[1] // (2 * HEAD)
    known = (request_adapter_index, lengths)
    own = jnp.concatenate([down_t, adapter_up_factor], axis=1).reshape(-1, width)
    gains = prepare(router_logit_scores.T, routes.T)

    if n_ex != 8 or n_dp != 4:
        context = attend(lengths, queries, rotated_key_heads, token_value_heads, 0, pairs)
        shard = lax.all_gather(attention_output_weight, "dp", axis=0, tiled=True)
        pool = lax.all_gather(own, "expert", axis=0, tiled=True)
        part = project(context, residual, [shard], [lambda z, i: z * 0])
        part = adapt(known, context, part, [pool], [lambda i: i * 0], rank)
        hidden0, send0 = close(part, context, expert_norm_scale, [], [])
        hidden1, send1 = close(part, context, expert_norm_scale, [], [], (hidden0, gains))
        every0 = lax.all_gather(send0, "expert", axis=0, tiled=True)
        every1 = lax.all_gather(send1, "expert", axis=0, tiled=True)
        parts = []
        for d in range(n_ex):
            of = slice(d * tokens, (d + 1) * tokens)
            parts.append(run_experts((every0[of], every1[of]), weights, lambda i, g: i))
        mixture = lax.psum_scatter(
            jnp.concatenate(parts, axis=0), "expert", scatter_dimension=0, tiled=True
        )
        return finish(hidden0, hidden1, [mixture])

    def beside(a):
        return lax.ppermute(a, "expert", [(e, e ^ 1) for e in range(n_ex)])

    def across(a):
        return lax.ppermute(a, "expert", [(e, e ^ (4 if e & 1 else 2)) for e in range(n_ex)])

    def turned(a):
        return lax.ppermute(a, "expert", [(e, e ^ (3 if e & 1 else 5)) for e in range(n_ex)])

    def along(a, step):
        sent = []
        for e in range(n_ex):
            for d in range(n_dp):
                to = d - 1 if e & 1 else d + 1
                origin = d + step - 1 if e & 1 else d - step + 1
                if 0 <= to < n_dp and 0 <= origin < n_dp:
                    sent.append((d * n_ex + e, to * n_ex + e))
        return lax.ppermute(a, ("dp", "expert"), sent)

    def after(a, *others):
        return lax.optimization_barrier((a, *others))[0]

    def first_row(step, side):
        def at(z, i):
            source = z + side * step * (1 - 2 * (i & 1))
            return jnp.where((source >= 0) & (source < n_dp), source * rows, -1)

        return at

    def attend_next(first, so_far, *others):
        q = after(queries, *others)
        return attend(lengths, q, rotated_key_heads, token_value_heads, first, 1, so_far)

    z1 = along(attention_output_weight, 1)
    pair_weights = [beside(w) for w in weights[:2]]
    p0 = across(own)
    other = beside(own)
    p1 = across(other)
    context = attend_next(0, None, pair_weights[0])
    z2 = along(after(z1, context), 2)
    p0_other = beside(after(p0, context))
    context = attend_next(1, context, pair_weights[1])
    pair_weights.append(beside(weights[2]))
    context = attend_next(2, context, pair_weights[2])
    context = attend_next(3, context)
    p2 = across(after(p0_other, p1))
    p1_other = beside(p1)
    z1_other, z2_other = beside(z1), beside(z2)
    z2_other = beside(after(z2, context))
    z3 = [along(z2[:, :cut], 3), along(z2[:, cut:], 3)]
    few = held * 3 // 4
    owners = [
        lambda i: i * held,
        lambda i: (i ^ 1) * held,
        lambda i: (i ^ (2 + 2 * (i & 1))) * held,
        lambda i: (i ^ (3 + 2 * (i & 1))) * held,
        lambda i: (i ^ (5 - 2 * (i & 1))) * held,
        lambda i: (i ^ (4 - 2 * (i & 1))) * held,
        lambda i: (i ^ 7) * held,
        lambda i: (i ^ 6) * held,
        lambda i: (i ^ 6) * held + few,
    ]
    part = project(
        context,
        residual,
        [attention_output_weight, z1, z1_other, z2, z2_other],
        [lambda z, i: z * rows] + [first_row(s, side) for s in (1, 2) for side in (-1, 1)],
    )
    p2_other = [beside(p2[: few * 2 * rank]), beside(p2[few * 2 * rank :])]
    pools = [own, other, p0, p1, p0_other, p1_other, p2, *p2_other]
    whole = adapt(known, context, part, pools, owners, rank)
    ends = [first_row(3, -1), first_row(3, 1)]
    task = functools.partial(close, whole, context, expert_norm_scale)
    hidden0, send0 = task([z3[0], beside(z3[0])], ends)
    other0 = beside(send0)
    near0, next0 = across(send0), across(other0)
    late = after(z3[1], send0)
    parts = [z3[1], beside(late[:, :cut]), beside(late[:, cut:])]
    hidden1, send1 = task(parts, [ends[0], ends[1], ends[1]], (hidden0, gains))
    near0_other = beside(near0)
    far0 = across(near0_other)
    other1 = beside(send1)
    near1, next1 = across(after(send1, near0_other)), across(other1)
    run = functools.partial(
        run_experts, weights=weights + tuple(pair_weights), spread=lambda i, g: i ^ g
    )
    home = run((send0, send1))
    far1 = across(beside(after(near1, next0, home)))
    r_near = run((near0, after(near1, home)))
    r_next = run((next0, after(next1, r_near)))
    back = across(r_next)
    r_far = run((far0, after(far1, r_next)))
    ready = beside(r_near)
    far_sum = across(r_far).astype(F32) + ready.astype(F32)
    back1 = beside(back)
    back0 = turned(far_sum.astype(BF16))
    rest = finish(hidden0, hidden1, [home, back1], F32)
    return (rest + back0.astype(F32)).astype(BF16)


def solution(mesh):
    return jax.shard_map(
        per_device,
        mesh=mesh,
        in_specs=(
            P(("dp", "expert"), None),
            P(("dp", "expert"), None),
            P(("dp", "expert"), None),
            P(("dp", "expert"), None),
            P(("dp", "expert"), None),
            P(("dp", "expert")),
            P("dp", None),
            P("expert", None, None),
            P("expert", None, None),
            P(),
            P(("dp", "expert"), None),
            P(("dp", "expert"), None),
            P("expert", None, None),
            P("expert", None, None),
            P("expert", None, None),
        ),
        out_specs=P(("dp", "expert"), None),
        check_vma=False,
    )
```

```python
import functools

import jax
import jax.numpy as jnp
from jax import lax
from jax.experimental import pallas as pl
from jax.experimental.pallas import tpu as pltpu
from jax.sharding import PartitionSpec as P

HEAD = 64
GROUPS = 3
BF16, F32 = jnp.bfloat16, jnp.float32
VMEM = pl.BlockSpec(memory_space=pltpu.VMEM)
SMEM = pl.BlockSpec(memory_space=pltpu.SMEM)
ANY = pl.BlockSpec(memory_space=pl.ANY)
MIB = 2**20


def call(kernel, name, out_shape, in_specs, out_specs, scratch, room, flops, **more):
    return pl.pallas_call(
        kernel,
        name=name,
        out_shape=out_shape,
        in_specs=in_specs,
        out_specs=out_specs,
        scratch_shapes=scratch,
        compiler_params=pltpu.CompilerParams(vmem_limit_bytes=room * MIB),
        cost_estimate=pl.CostEstimate(flops=flops, bytes_accessed=1024, transcendentals=0),
        **more,
    )


def attend_kernel(lengths_ref, q_ref, k_ref, v_ref, *refs):
    o_ref, bias = refs[-2:]
    tokens = q_ref.shape[0]
    half = tokens // 2

    @pl.when(pl.program_id(0) == 0)
    def _():
        row = lax.broadcasted_iota(jnp.int32, (tokens, tokens), 0)
        col = lax.broadcasted_iota(jnp.int32, (tokens, tokens), 1)
        same = row >= col
        end = 0
        for r in range(lengths_ref.shape[1]):
            end = end + lengths_ref[0, r]
            same = same & ((row < end) | (col >= end))
        bias[...] = jnp.where(same, 0.0, -1e30)

    for j in range(k_ref.shape[1] // HEAD):
        keys = k_ref[:, j * HEAD : (j + 1) * HEAD]
        values = v_ref[:, j * HEAD : (j + 1) * HEAD]
        for g in range(GROUPS):
            at = (j * GROUPS + g) * HEAD
            q = q_ref[:, at : at + HEAD] * jnp.asarray(HEAD**-0.5, BF16)
            for first, seen in ((0, half), (half, tokens)):
                s = lax.dot_general(
                    q[first : first + half],
                    keys[:seen],
                    (((1,), (1,)), ((), ())),
                    preferred_element_type=F32,
                )
                s = s + bias[first : first + half, :seen]
                p = jnp.exp(s - jnp.max(s, axis=-1, keepdims=True))
                w = (p * (1.0 / jnp.sum(p, axis=-1, keepdims=True))).astype(BF16)
                o = jnp.dot(w, values[:seen], preferred_element_type=F32)
                o_ref[first : first + half, at : at + HEAD] = o.astype(BF16)


def attend(lengths, q, k, v, first, pairs, so_far=None):
    tokens = q.shape[0]
    wide = 2 * GROUPS * HEAD
    return pl.pallas_call(
        attend_kernel,
        name="attend",
        grid=(pairs,),
        out_shape=jax.ShapeDtypeStruct(q.shape, BF16),
        in_specs=[
            SMEM,
            pl.BlockSpec((tokens, wide), lambda i: (0, first + i)),
            pl.BlockSpec((tokens, 2 * HEAD), lambda i: (0, first + i)),
            pl.BlockSpec((tokens, 2 * HEAD), lambda i: (0, first + i)),
        ]
        + ([ANY] if so_far is not None else []),
        out_specs=pl.BlockSpec((tokens, wide), lambda i: (0, first + i)),
        scratch_shapes=[pltpu.VMEM((tokens, tokens), F32)],
        compiler_params=pltpu.CompilerParams(vmem_limit_bytes=8 * MIB),
        cost_estimate=pl.CostEstimate(flops=10**9, bytes_accessed=1024, transcendentals=0),
        input_output_aliases={4: 0} if so_far is not None else {},
    )(lengths, q, k, v, *([so_far] if so_far is not None else []))


GATES, SPAN = 32, 128


def prepare_kernel(logits_ref, routes_ref, gain_ref):
    top, tokens = logits_ref.shape
    logits = logits_ref[...]
    raised = jnp.exp(logits - jnp.max(logits, axis=0, keepdims=True))
    gates = raised / jnp.sum(raised, axis=0, keepdims=True)
    expert = lax.broadcasted_iota(jnp.int32, (GATES, tokens), 0)
    gain = jnp.zeros((GATES, tokens), F32)
    for j in range(top):
        gain = gain + jnp.where(expert == routes_ref[j : j + 1], gates[j : j + 1], 0.0)
    high = gain.astype(BF16).astype(F32)
    rest = jnp.zeros((SPAN - 2 * GATES, tokens), F32)
    gain_ref[...] = jnp.concatenate([high, gain - high, rest], axis=0).T.astype(BF16)


def prepare(logits, routes):
    return call(
        prepare_kernel,
        "prepare",
        jax.ShapeDtypeStruct((logits.shape[1], SPAN), BF16),
        [VMEM] * 2,
        VMEM,
        [],
        4,
        10**9,
    )(logits, routes)


def project_kernel(sources, ctx_ref, res_ref, *refs):
    shard, part_ref = refs[:-1], refs[-1]
    z, i = lax.axis_index("dp"), lax.axis_index("expert")
    part_ref[...] = res_ref[...].astype(F32)
    for source, piece in zip(sources, shard):
        add_shard(source(z, i), ctx_ref, piece, part_ref)


def adapt_kernel(owners, rank, *refs):
    ids, lengths, ctx_ref, part_ref = refs[:4]
    pool = refs[4:-4]
    out_ref, low_s, up_s, sem = refs[-4:]
    requests = ids.shape[0]
    i = lax.axis_index("expert")

    def copies(r, ref, first):
        return [
            pltpu.make_async_copy(
                ref.at[pl.ds(first + h * rank, rank)], to.at[pl.ds(r * rank, rank)], sem.at[r, h]
            )
            for h, to in ((0, low_s), (1, up_s))
        ]

    for r in range(requests):
        for k, owner in enumerate(owners):
            at = ids[r] - owner(i)

            @pl.when((at >= 0) & (at < pool[k].shape[0] // (2 * rank)))
            def _():
                for c in copies(r, pool[k], pl.multiple_of(at * (2 * rank), 2 * rank)):
                    c.start()

    for r in range(requests):
        for c in copies(r, pool[0], 0):
            c.wait()
    low = lax.dot_general(
        ctx_ref[...], low_s[...], (((1,), (1,)), ((), ())), preferred_element_type=F32
    )
    row = lax.broadcasted_iota(jnp.int32, low.shape, 0)
    lane = lax.broadcasted_iota(jnp.int32, low.shape, 1)
    end = 0
    mine = lane < 0
    for r in range(requests):
        start, end = end, end + lengths[0, r]
        inside = (row >= start) & (row < end)
        mine = mine | (inside & (lane >= r * rank) & (lane < (r + 1) * rank))
    low = jnp.where(mine, low, 0.0).astype(BF16)
    out_ref[...] = part_ref[...] + jnp.dot(low, up_s[...], preferred_element_type=F32)


def add_shard(at, ctx_ref, piece, total_ref):
    @pl.when(at >= 0)
    def _():
        first = pl.multiple_of(at, 128)
        total_ref[...] += jnp.dot(
            ctx_ref[:, pl.ds(first, piece.shape[0])], piece[...], preferred_element_type=F32
        )


def project(ctx, residual, shards, sources):
    return call(
        functools.partial(project_kernel, sources),
        "project",
        jax.ShapeDtypeStruct(residual.shape, F32),
        [VMEM] * (2 + len(shards)),
        VMEM,
        [],
        8,
        10**9,
    )(ctx, residual, *shards)


def adapt(known, ctx, part, pools, owners, rank):
    requests, width = known[0].shape[0], part.shape[1]
    return call(
        functools.partial(adapt_kernel, owners, rank),
        "adapt",
        jax.ShapeDtypeStruct(part.shape, F32),
        [SMEM] * 2 + [VMEM] * 2 + [ANY] * len(pools),
        VMEM,
        [
            pltpu.VMEM((requests * rank, width), BF16),
            pltpu.VMEM((requests * rank, width), BF16),
            pltpu.SemaphoreType.DMA((requests, 2)),
        ],
        8,
        10**9,
    )(*known, ctx, part, *pools)


def first_columns(width):
    return max(128, width // 384 * 128)


def close_kernel(sources, column, second, *refs):
    part_ref, ctx_ref, scale_ref = refs[:3]
    shard = refs[3 : 3 + len(sources)]
    hidden_ref, send_ref = refs[-2:]
    tokens, width = hidden_ref.shape
    z, i = lax.axis_index("dp"), lax.axis_index("expert")
    hidden_ref[...] = part_ref[:, column : column + width]
    beside = 0
    for source, piece in zip(sources, shard):
        wide = piece.shape[1]
        add_shard(source(z, i), ctx_ref, piece, hidden_ref.at[:, beside : beside + wide])
        beside = (beside + wide) % width
    h = hidden_ref[...]
    scale = scale_ref[...].reshape(1, -1)[:, column : column + width]
    send_ref[:, :width] = (h * scale).astype(BF16)
    if second:
        left_ref, gain_ref = refs[3 + len(sources) : -2]
        left = left_ref[...]
        square = jnp.sum(h * h, axis=-1, keepdims=True)
        square = square + jnp.sum(left * left, axis=-1, keepdims=True)
        inv = lax.rsqrt(square * (1.0 / ctx_ref.shape[1]) + 1e-06)
        high = inv.astype(BF16).astype(F32)
        lane = lax.broadcasted_iota(jnp.int32, (tokens, SPAN), 1)
        gain = gain_ref[...].astype(F32)
        gain = jnp.where(lane == 2 * GATES, high, gain)
        gain = jnp.where(lane == 2 * GATES + 1, inv - high, gain)
        send_ref[:, width:] = gain.astype(BF16)


def close(part, ctx, scale, shards, sources, left=()):
    tokens, width = part.shape
    second = len(left) > 0
    cut = first_columns(width)
    mine = width - cut if second else cut
    return call(
        functools.partial(close_kernel, sources, cut if second else 0, second),
        "close",
        (
            jax.ShapeDtypeStruct((tokens, mine), F32),
            jax.ShapeDtypeStruct((tokens, mine + SPAN if second else mine), BF16),
        ),
        [VMEM] * (3 + len(shards) + len(left)),
        (VMEM, VMEM),
        [],
        8,
        10**9,
    )(part, ctx, scale, *shards, *left)


def experts_kernel(groups, spread, a_ref, b_ref, *refs):
    w, out_ref = refs[: 3 * groups], refs[3 * groups]
    total_ref, x_ref = refs[3 * groups + 1 :]
    local = w[0].shape[0]
    cut, wide = a_ref.shape[1], b_ref.shape[1] - SPAN
    i = lax.axis_index("expert")
    x_ref[:, :cut] = a_ref[...]
    x_ref[:, cut:] = b_ref[:, :wide]
    strip = b_ref[:, wide:].astype(F32)
    lane = lax.broadcasted_iota(jnp.int32, strip.shape, 1)
    inv = strip[:, 2 * GATES : 2 * GATES + 1] + strip[:, 2 * GATES + 1 : 2 * GATES + 2]
    for e in range(groups * local):
        g, own = divmod(e, local)
        number = spread(i, g) * local + own
        mine = (lane == number) | (lane == number + GATES)
        coef = jnp.sum(jnp.where(mine, strip, 0.0), axis=-1, keepdims=True)
        gate = jnp.dot(x_ref[...], w[3 * g][own], preferred_element_type=F32) * inv
        up = jnp.dot(x_ref[...], w[3 * g + 1][own], preferred_element_type=F32)
        act = (gate / (1.0 + jnp.exp(-gate)) * (up * (inv * coef))).astype(BF16)
        down = jnp.dot(act, w[3 * g + 2][own], preferred_element_type=F32)
        if e == 0:
            total_ref[...] = down
        elif e < groups * local - 1:
            total_ref[...] += down
        else:
            out_ref[...] = (total_ref[...] + down).astype(BF16)


def run_experts(x, weights, spread):
    a, b = x
    groups = len(weights) // 3
    tokens, width = a.shape[0], weights[0].shape[1]
    return call(
        functools.partial(experts_kernel, groups, spread),
        "experts",
        jax.ShapeDtypeStruct((tokens, width), BF16),
        [VMEM] * (2 + 3 * groups),
        VMEM,
        [pltpu.VMEM((tokens, width), F32), pltpu.VMEM((tokens, width), BF16)],
        12,
        10**9,
    )(a, b, *weights)


def finish_kernel(left_ref, right_ref, *refs):
    parts, out_ref = refs[:-1], refs[-1]
    at = 0
    for hidden in (left_ref, right_ref):
        to = at + hidden.shape[1]
        total = hidden[...]
        for p in parts:
            total = total + p[:, at:to].astype(F32)
        out_ref[:, at:to] = total.astype(out_ref.dtype)
        at = to


def finish(left, right, parts, kind=BF16):
    return call(
        finish_kernel,
        "finish",
        jax.ShapeDtypeStruct(parts[0].shape, kind),
        [VMEM] * (2 + len(parts)),
        VMEM,
        [],
        8,
        10**9,
    )(left, right, *parts)


def per_device(
    queries,
    rotated_key_heads,
    token_value_heads,
    residual,
    lengths,
    request_adapter_index,
    attention_output_weight,
    adapter_down_factor,
    adapter_up_factor,
    expert_norm_scale,
    router_logit_scores,
    routes,
    expert_gate_weight,
    expert_up_weight,
    expert_down_weight,
):
    tokens = queries.shape[0]
    rank = adapter_up_factor.shape[1]
    held = adapter_up_factor.shape[0]
    n_dp, n_ex = lax.axis_size("dp"), lax.axis_size("expert")
    rows, width = attention_output_weight.shape
    cut = first_columns(width)
    down_t = jnp.swapaxes(adapter_down_factor, 1, 2)
    weights = (expert_gate_weight, expert_up_weight, expert_down_weight)
    pairs = rotated_key_heads.shape[1] // (2 * HEAD)
    known = (request_adapter_index, lengths)
    own = jnp.concatenate([down_t, adapter_up_factor], axis=1).reshape(-1, width)
    gains = prepare(router_logit_scores.T, routes.T)

    if n_ex != 8 or n_dp != 4:
        context = attend(lengths, queries, rotated_key_heads, token_value_heads, 0, pairs)
        shard = lax.all_gather(attention_output_weight, "dp", axis=0, tiled=True)
        pool = lax.all_gather(own, "expert", axis=0, tiled=True)
        part = project(context, residual, [shard], [lambda z, i: z * 0])
        part = adapt(known, context, part, [pool], [lambda i: i * 0], rank)
        hidden0, send0 = close(part, context, expert_norm_scale, [], [])
        hidden1, send1 = close(part, context, expert_norm_scale, [], [], (hidden0, gains))
        every0 = lax.all_gather(send0, "expert", axis=0, tiled=True)
        every1 = lax.all_gather(send1, "expert", axis=0, tiled=True)
        parts = []
        for d in range(n_ex):
            of = slice(d * tokens, (d + 1) * tokens)
            parts.append(run_experts((every0[of], every1[of]), weights, lambda i, g: i))
        mixture = lax.psum_scatter(
            jnp.concatenate(parts, axis=0), "expert", scatter_dimension=0, tiled=True
        )
        return finish(hidden0, hidden1, [mixture])

    def beside(a):
        return lax.ppermute(a, "expert", [(e, e ^ 1) for e in range(n_ex)])

    def across(a):
        return lax.ppermute(a, "expert", [(e, e ^ (4 if e & 1 else 2)) for e in range(n_ex)])

    def turned(a):
        return lax.ppermute(a, "expert", [(e, e ^ (3 if e & 1 else 5)) for e in range(n_ex)])

    def along(a, step):
        sent = []
        for e in range(n_ex):
            for d in range(n_dp):
                to = d - 1 if e & 1 else d + 1
                origin = d + step - 1 if e & 1 else d - step + 1
                if 0 <= to < n_dp and 0 <= origin < n_dp:
                    sent.append((d * n_ex + e, to * n_ex + e))
        return lax.ppermute(a, ("dp", "expert"), sent)

    def after(a, *others):
        return lax.optimization_barrier((a, *others))[0]

    def first_row(step, side):
        def at(z, i):
            source = z + side * step * (1 - 2 * (i & 1))
            return jnp.where((source >= 0) & (source < n_dp), source * rows, -1)

        return at

    def attend_next(first, so_far, *others):
        q = after(queries, *others)
        return attend(lengths, q, rotated_key_heads, token_value_heads, first, 1, so_far)

    z1 = along(attention_output_weight, 1)
    pair_weights = [beside(w) for w in weights[:2]]
    p0 = across(own)
    other = beside(own)
    p1 = turned(own)
    context = attend_next(0, None, pair_weights[0])
    z2 = along(after(z1, context), 2)
    p0_other = beside(after(p0, context))
    context = attend_next(1, context, pair_weights[1])
    pair_weights.append(beside(weights[2]))
    context = attend_next(2, context, pair_weights[2])
    context = attend_next(3, context)
    p2 = across(after(p0_other, p1))
    p1_other = beside(p1)
    z1_other, z2_other = beside(z1), beside(z2)
    z2_other = beside(after(z2, context))
    z3 = [along(z2[:, :cut], 3), along(z2[:, cut:], 3)]
    few = held * 3 // 4
    owners = [
        lambda i: i * held,
        lambda i: (i ^ 1) * held,
        lambda i: (i ^ (2 + 2 * (i & 1))) * held,
        lambda i: (i ^ (3 + 2 * (i & 1))) * held,
        lambda i: (i ^ (5 - 2 * (i & 1))) * held,
        lambda i: (i ^ (4 - 2 * (i & 1))) * held,
        lambda i: (i ^ 7) * held,
        lambda i: (i ^ 6) * held,
        lambda i: (i ^ 6) * held + few,
    ]
    part = project(
        context,
        residual,
        [attention_output_weight, z1, z1_other, z2, z2_other],
        [lambda z, i: z * rows] + [first_row(s, side) for s in (1, 2) for side in (-1, 1)],
    )
    p2_other = [beside(p2[: few * 2 * rank]), beside(p2[few * 2 * rank :])]
    pools = [own, other, p0, p1, p0_other, p1_other, p2, *p2_other]
    whole = adapt(known, context, part, pools, owners, rank)
    ends = [first_row(3, -1), first_row(3, 1)]
    task = functools.partial(close, whole, context, expert_norm_scale)
    hidden0, send0 = task([z3[0], beside(z3[0])], ends)
    other0 = beside(send0)
    near0, next0 = across(send0), across(other0)
    late = after(z3[1], send0)
    parts = [z3[1], beside(late[:, :cut]), beside(late[:, cut:])]
    hidden1, send1 = task(parts, [ends[0], ends[1], ends[1]], (hidden0, gains))
    near0_other = beside(near0)
    far0 = across(near0_other)
    other1 = beside(send1)
    near1, next1 = across(after(send1, near0_other)), across(other1)
    run = functools.partial(
        run_experts, weights=weights + tuple(pair_weights), spread=lambda i, g: i ^ g
    )
    home = run((send0, send1))
    far1 = across(beside(after(near1, next0, home)))
    r_near = run((near0, after(near1, home)))
    r_next = run((next0, after(next1, r_near)))
    back = across(r_next)
    r_far = run((far0, after(far1, r_next)))
    ready = beside(r_near)
    far_sum = across(r_far).astype(F32) + ready.astype(F32)
    back1 = beside(back)
    back0 = turned(far_sum.astype(BF16))
    rest = finish(hidden0, hidden1, [home, back1], F32)
    return (rest + back0.astype(F32)).astype(BF16)


def solution(mesh):
    return jax.shard_map(
        per_device,
        mesh=mesh,
        in_specs=(
            P(("dp", "expert"), None),
            P(("dp", "expert"), None),
            P(("dp", "expert"), None),
            P(("dp", "expert"), None),
            P(("dp", "expert"), None),
            P(("dp", "expert")),
            P("dp", None),
            P("expert", None, None),
            P("expert", None, None),
            P(),
            P(("dp", "expert"), None),
            P(("dp", "expert"), None),
            P("expert", None, None),
            P("expert", None, None),
            P("expert", None, None),
        ),
        out_specs=P(("dp", "expert"), None),
        check_vma=False,
    )
```
